512 devices in a mesh: sx: 8 (over y), sy: 8 (over x, z_hi), ch: 8 (over z_lo, core).
Axes of the slice: x: 4, y: 8, z: 8 (z_hi: 2, z_lo: 4; z = z_hi * 4 + z_lo), core: 2. Of those that a mesh axis runs over, the one named last changes fastest.
Arguments:
- volume: bfloat16 [128, 2, 256, 1024], P('ch', None, 'sx', 'sy'), may hold values from -6 to 6
- weights: bfloat16 [128, 128, 3, 3, 3], P('ch'), may hold values from -0.109375 to 0.109375
- bias: float32 [128], P('ch'), may hold values from -3 to 3
Outputs:
- activated: bfloat16 [128, 2, 256, 1024], P('ch', None, 'sx', 'sy')
The draws below stay inside these ranges and needn't reach their ends.
All inputs are finite; a program needn't handle non-finite values.
Results may differ from the reference program's by a relative error of at most 0.0065.
Values may be sent and summed in bfloat16 or wider, within the bound.
No kernel may reach another device: no remote copies, remote signals or barrier semaphores. Data moves between devices by JAX's collectives and lax.ppermute only.
A program may use at most 64 MiB of HBM per device.

```python
import jax
import jax.numpy as jnp
from jax import lax

C = 128
DZ = 2
NX = 256
NY = 1024


def level_of(stream_key, shape, pieces, low, top_value):
    level = 1.0
    for position, parts in pieces:
        steps = jax.random.uniform(jax.random.fold_in(jax.random.fold_in(stream_key, 6), position), (parts,), jnp.float32, low / len(pieces), top_value / len(pieces))
        level = level * jnp.repeat(jnp.exp(steps), shape[position] // parts).reshape((-1,) + (1,) * (len(shape) - 1 - position))
    return level


def centred(key, shape, scale, limit, split=(), held_as=jnp.bfloat16):
    array = jax.random.normal(key, shape, jnp.float32) * scale
    if len(split) > 0:
        array = level_of(key, shape, split, -0.22, 0.18) * array
    return jnp.clip(array, min=-limit, max=limit).astype(held_as)


def setup_inputs(seed: int = 0) -> dict:
    arg_keys = jax.random.split(jax.random.key(seed), 4)
    volume = centred(arg_keys[0], (C, DZ, NX, NY), 1.0, 6.0, ((0, 8), (2, 8), (3, 8)))
    weights = centred(arg_keys[1], (C, C, 3, 3, 3), (27 * C) ** -0.5, 0.109375, ((0, 8),))
    bias = centred(arg_keys[2], (C,), 0.5, 3.0, ((0, 8),), jnp.float32)
    return {"volume": volume, "weights": weights, "bias": bias}


def reference(volume, weights, bias):
    pre = lax.conv_general_dilated(volume[None], weights, (1, 1, 1), "SAME", dimension_numbers=("NCDHW", "OIDHW", "NCDHW"), preferred_element_type=jnp.float32)[0]
    pre = pre + bias.astype(jnp.float32)[:, None, None, None]
    return jnp.where(pre >= 0, pre, 0.3 * pre).astype(jnp.bfloat16)
```

```python
import jax
import jax.numpy as jnp
from jax import lax
from jax.experimental import pallas as pl
from jax.experimental.pallas import tpu as pltpu
from jax.sharding import PartitionSpec as P

BF = jnp.bfloat16
F32 = jnp.float32
SETS = [[0, 1, 2, 3], [4, 5, 6, 7]]


def call(kernel, out_shapes, scratch, *args, flops=0, moved=0):
    vmem = pl.BlockSpec(memory_space=pltpu.VMEM)
    many = isinstance(out_shapes, (list, tuple))
    return pl.pallas_call(
        kernel,
        out_shape=out_shapes,
        in_specs=[vmem] * len(args),
        out_specs=[vmem] * len(out_shapes) if many else vmem,
        scratch_shapes=scratch,
        cost_estimate=pl.CostEstimate(flops=flops, bytes_accessed=moved, transcendentals=0),
    )(*args)


def shaped(*shape, dtype=BF):
    return jax.ShapeDtypeStruct(shape, dtype)


def lanes_of(shape):
    return lax.broadcasted_iota(jnp.int32, shape, len(shape) - 1)


def pack_kernel(vol, slabs, rows, edges, cols, flat):
    flat[...] = vol[...].reshape(1024, 128).astype(F32)
    for z in range(2):
        for row in range(32):
            tile = flat[pl.ds(z * 32 + row, 16, stride=64), :].astype(BF)
            q, r = divmod(row, 8)
            slabs[q, z * 8 + r] = tile
            slabs[q + 4, z * 8 + r] = tile
            here = pl.ds(z * 16, 16)
            if row == 0:
                rows[0, here] = tile
            if row == 31:
                rows[1, here] = tile
            if r == 7 and q < 3:
                edges[q + 1, here] = tile
            if r == 0 and q > 0:
                edges[q - 1, pl.ds(32 + z * 16, 16)] = tile
    nothing = jnp.zeros((32, 128), BF)
    edges[0, pl.ds(0, 32)] = nothing
    edges[3, pl.ds(32, 32)] = nothing
    lane = lanes_of((32, 128))
    both = jnp.zeros((32, 128), F32)
    for z in range(2):
        for c in range(16):
            tile = flat[pl.ds(c * 64 + z * 32, 32), :]
            j = z * 16 + c
            both = jnp.where(lane == j, pltpu.roll(tile, j, 1) if j else tile, both)
            both = jnp.where(lane == 32 + j, pltpu.roll(tile, 33 + j, 1), both)
    cols[...] = both


def corner_kernel(cols, top, bottom, side, buf):
    both = jnp.concatenate(
        [top[...].astype(F32), bottom[...].astype(F32), jnp.zeros((64, 128), F32)], axis=0
    )
    turned = both.T
    first, last = turned[0:1, :], turned[127:128, :]
    lane = lanes_of((1, 128))
    buf[...] = jnp.zeros((40, 128), F32)
    buf[pl.ds(1, 32), :] = cols[...]
    buf[pl.ds(0, 1), :] = jnp.where(lane < 32, first, pltpu.roll(last, 32, 1))
    buf[pl.ds(33, 1), :] = jnp.where(lane < 32, pltpu.roll(first, 96, 1), last)
    side[...] = buf[...].astype(BF)


def halo_kernel(edges, top, bottom, left, right, out):
    lane = lanes_of((40, 128))
    beside = jnp.where(
        lane < 32,
        pltpu.roll(left[...].astype(F32), 96, 1),
        pltpu.roll(right[...].astype(F32), 32, 1),
    )
    for d in range(8):
        q = d % 4
        above = top[...] if q == 0 else edges[q, pl.ds(0, 32)]
        below = bottom[...] if q == 3 else edges[q, pl.ds(32, 32)]
        out[d, pl.ds(0, 32)] = above
        out[d, pl.ds(32, 32)] = below
        out[d, pl.ds(64, 16)] = beside[8 * q : 8 * q + 16].astype(BF)


def conv_kernel(slabs, halo, filters, out, field, taps):
    for src in range(8):
        for z in range(2):
            at = z * 128 + src * 16
            field[pl.ds(at, 16), :] = halo[src, pl.ds(z * 16, 16)]
            field[pl.ds(9 * 256 + at, 16), :] = halo[src, pl.ds(32 + z * 16, 16)]
            for r in range(8):
                field[pl.ds((r + 1) * 256 + at, 16), :] = slabs[src, z * 8 + r]
    for e in range(3):
        for zo in range(2):
            for s in range(4):
                for b in range(3):
                    for zi in range(2):
                        tap = (zi - zo + 1) * 9 + b * 3 + e
                        taps[pl.ds(e * 128 + zo * 64 + s * 16, 16), pl.ds(b * 256 + zi * 128, 128)] = filters[
                            s, pl.ds(tap * 16, 16)
                        ]
    parts = jnp.concatenate([filters[s, pl.ds(432, 16)].astype(F32) for s in range(4)], axis=0)
    offset = (parts[:, 0:1] + parts[:, 1:2]) + parts[:, 2:3]
    offset = jnp.concatenate([offset, offset], axis=0)
    lane16 = lanes_of((16, 128))
    sides = []
    for side in range(2):
        depths = []
        for z in range(2):
            total = jnp.zeros((16, 128), F32)
            for src in range(8):
                piece = halo[src, pl.ds(64, 16)].astype(F32)
                shift = (src * 16 - (side * 32 + z * 16)) % 128
                piece = pltpu.roll(piece, shift, 1) if shift else piece
                total = jnp.where(lane16 // 16 == src, piece, total)
            depths.append(total)
        sides.append(jnp.concatenate(depths, axis=1))
    beside = jnp.concatenate(
        [jnp.concatenate([sides[0][b : b + 8], sides[1][b : b + 8]], axis=0) for b in range(3)], axis=1
    ).astype(BF)
    weights = taps[...]
    edge = lax.dot_general(weights, beside, (((1,), (1,)), ((), ())), preferred_element_type=F32)
    lane = lanes_of((128, 128))
    for p in range(4):
        r = 2 * p
        pair = jnp.concatenate(
            [field[pl.ds(r * 256, 768), :], field[pl.ds((r + 1) * 256, 768), :]], axis=1
        )
        total = jnp.dot(weights, pair, preferred_element_type=F32)
        for h in range(2):
            at = slice(h * 128, (h + 1) * 128)
            row = r + h
            before = pltpu.roll(total[0:128, at], 1, 1)
            after = pltpu.roll(total[256:384, at], 127, 1)
            pre = total[128:256, at]
            pre = pre + jnp.where(lane == 0, edge[0:128, row : row + 1], before)
            pre = pre + jnp.where(lane == 127, edge[256:384, 8 + row : 9 + row], after)
            pre = pre + offset
            done = jnp.where(pre >= 0, pre, 0.3 * pre).astype(BF)
            for z in range(2):
                for s in range(4):
                    out[s, z * 8 + row] = done[z * 64 + s * 16 : z * 64 + s * 16 + 16]


def unpack_kernel(got, out, flat):
    for q in range(4):
        for z in range(2):
            for r in range(8):
                flat[pl.ds(z * 32 + q * 8 + r, 16, stride=64), :] = got[q, z * 8 + r].astype(F32)
    out[...] = flat[...].reshape(16, 2, 32, 128).astype(BF)


def shifts(array, axis, up=True):
    size = lax.axis_size(axis)
    pairs = [(i, i + 1) for i in range(size - 1)]
    return lax.ppermute(array, axis, pairs if up else [(j, i) for i, j in pairs])


def thirds(bias):
    high = bias.astype(BF)
    rest = bias - high.astype(F32)
    middle = rest.astype(BF)
    low = (rest - middle.astype(F32)).astype(BF)
    return jnp.pad(jnp.stack([high, middle, low], axis=1), ((0, 0), (0, 125)))


def per_device(volume, weights, bias):
    slabs, rows, edges, cols = call(
        pack_kernel,
        [shaped(8, 16, 16, 128), shaped(2, 32, 128), shaped(4, 64, 128), shaped(32, 128, dtype=F32)],
        [pltpu.VMEM((1024, 128), F32)],
        volume,
        moved=1 << 20,
    )
    top = shifts(rows[1], "sx", True)
    bottom = shifts(rows[0], "sx", False)
    slabs = lax.all_to_all(slabs, "ch", split_axis=0, concat_axis=0, tiled=True)
    own = jnp.concatenate([weights.transpose(2, 3, 4, 0, 1).reshape(432, 128), thirds(bias)], axis=0)
    filters = lax.all_to_all(
        jnp.broadcast_to(own, (4, 448, 128)), "ch", split_axis=0, concat_axis=0, tiled=True, axis_index_groups=SETS
    )
    side = call(corner_kernel, shaped(40, 128), [pltpu.VMEM((40, 128), F32)], cols, top, bottom, moved=1 << 16)
    left = shifts(side, "sy", True)
    right = shifts(side, "sy", False)
    halo = call(halo_kernel, shaped(8, 80, 128), [], edges, top, bottom, left, right, moved=1 << 18)
    halo = lax.all_to_all(halo, "ch", split_axis=0, concat_axis=0, tiled=True)
    result = call(
        conv_kernel,
        shaped(4, 16, 16, 128),
        [pltpu.VMEM((2560, 128), BF), pltpu.VMEM((384, 768), BF)],
        slabs,
        halo,
        filters,
        flops=2 * 384 * 768 * 1024,
        moved=3 << 20,
    )
    result = lax.all_to_all(result, "ch", split_axis=0, concat_axis=0, tiled=True, axis_index_groups=SETS)
    return call(unpack_kernel, shaped(16, 2, 32, 128), [pltpu.VMEM((1024, 128), F32)], result, moved=1 << 19)


def solution(mesh):
    in_specs = (P("ch", None, "sx", "sy"), P("ch", None, None, None, None), P("ch"))
    out_specs = P("ch", None, "sx", "sy")
    return jax.shard_map(
        per_device, mesh=mesh, in_specs=in_specs, out_specs=out_specs, check_vma=False
    )
```

```python
import jax
import jax.numpy as jnp
from jax import lax
from jax.experimental import pallas as pl
from jax.experimental.pallas import tpu as pltpu
from jax.sharding import PartitionSpec as P


BF = jnp.bfloat16
F32 = jnp.float32
GRANT = 16 << 20


def call(kernel, out_shapes, scratch, *args, flops=0, moved=0):
    vmem = pl.BlockSpec(memory_space=pltpu.VMEM)
    many = isinstance(out_shapes, (list, tuple))
    return pl.pallas_call(
        kernel,
        out_shape=out_shapes,
        in_specs=[vmem] * len(args),
        out_specs=[vmem] * len(out_shapes) if many else vmem,
        scratch_shapes=scratch,
        cost_estimate=pl.CostEstimate(flops=flops, bytes_accessed=moved, transcendentals=0),
        compiler_params=pltpu.CompilerParams(vmem_limit_bytes=GRANT),
    )(*args)


def shaped(*shape, dtype=BF):
    return jax.ShapeDtypeStruct(shape, dtype)


def lanes_of(shape):
    return lax.broadcasted_iota(jnp.int32, shape, len(shape) - 1)


def pack_kernel(vol, slabs, first, last, edges, flat):
    flat[...] = vol[...].reshape(1024, 128).astype(F32)
    for z in range(2):
        for row in range(32):
            tile = flat[pl.ds(z * 32 + row, 16, stride=64), :].astype(BF)
            q, r = divmod(row, 8)
            slabs[q, z * 8 + r] = tile
            slabs[q + 4, z * 8 + r] = tile
            here = pl.ds(z * 16, 16)
            if row == 0:
                first[here] = tile
            if row == 31:
                last[here] = tile
            if r == 7 and q < 3:
                edges[q + 1, here] = tile
            if r == 0 and q > 0:
                edges[q - 1, pl.ds(32 + z * 16, 16)] = tile
    nothing = jnp.zeros((32, 128), BF)
    edges[0, pl.ds(0, 32)] = nothing
    edges[3, pl.ds(32, 32)] = nothing


def columns_kernel(vol, cols):
    lane = lanes_of((32, 128))
    both = jnp.zeros((32, 128), F32)
    for z in range(2):
        for c in range(16):
            tile = vol[c, z].astype(F32)
            j = z * 16 + c
            both = jnp.where(lane == j, pltpu.roll(tile, j, 1) if j else tile, both)
            both = jnp.where(lane == 32 + j, pltpu.roll(tile, 33 + j, 1), both)
    cols[...] = both


def corner_kernel(cols, top, bottom, side, buf):
    both = jnp.concatenate(
        [top[...].astype(F32), bottom[...].astype(F32), jnp.zeros((64, 128), F32)], axis=0
    )
    turned = both.T
    first, last = turned[0:1, :], turned[127:128, :]
    lane = lanes_of((1, 128))
    buf[...] = jnp.zeros((40, 128), F32)
    buf[pl.ds(1, 32), :] = cols[...]
    buf[pl.ds(0, 1), :] = jnp.where(lane < 32, first, pltpu.roll(last, 32, 1))
    buf[pl.ds(33, 1), :] = jnp.where(lane < 32, pltpu.roll(first, 96, 1), last)
    side[...] = buf[...].astype(BF)


def halo_kernel(edges, top, bottom, left, right, out):
    lane = lanes_of((40, 128))
    beside = jnp.where(
        lane < 32,
        pltpu.roll(left[...].astype(F32), 96, 1),
        pltpu.roll(right[...].astype(F32), 32, 1),
    )
    for d in range(8):
        q = d % 4
        above = top[...] if q == 0 else edges[q, pl.ds(0, 32)]
        below = bottom[...] if q == 3 else edges[q, pl.ds(32, 32)]
        out[d, pl.ds(0, 32)] = above
        out[d, pl.ds(32, 32)] = below
        out[d, pl.ds(64, 16)] = beside[8 * q : 8 * q + 16].astype(BF)


def inner_kernel(slabs, f0, f1, f2, f3, pre, taps, field):
    for src in range(8):
        for z in range(2):
            for r in range(8):
                field[pl.ds(r * 256 + z * 128 + src * 16, 16), :] = slabs[src, z * 8 + r]
    for e in range(3):
        for zo in range(2):
            for t, own in enumerate((f0, f1, f2, f3)):
                for b in range(3):
                    for zi in range(2):
                        tap = (zi - zo + 1) * 9 + b * 3 + e
                        taps[
                            pl.ds(e * 128 + zo * 64 + t * 16, 16), pl.ds(b * 256 + zi * 128, 128)
                        ] = own[pl.ds(tap * 16, 16)]
    weights = taps[...]
    lane = lanes_of((128, 128))
    for p in range(4):
        r = 2 * p
        low = 256 if r == 0 else 0
        high = 512 if r == 6 else 768
        start = (r - 1) * 256
        one = field[pl.ds(start + low, 768 - low), :]
        two = field[pl.ds(start + 256, high), :]
        if low:
            total = jnp.concatenate(
                [
                    jnp.dot(weights[:, low:], one, preferred_element_type=F32),
                    jnp.dot(weights, two, preferred_element_type=F32),
                ],
                axis=1,
            )
        elif high < 768:
            total = jnp.concatenate(
                [
                    jnp.dot(weights, one, preferred_element_type=F32),
                    jnp.dot(weights[:, :high], two, preferred_element_type=F32),
                ],
                axis=1,
            )
        else:
            total = jnp.dot(weights, jnp.concatenate([one, two], axis=1), preferred_element_type=F32)
        for h in range(2):
            pre[r + h] = aligned(total[:, h * 128 : (h + 1) * 128], lane)


def aligned(total, lane):
    before = jnp.where(lane == 0, 0.0, pltpu.roll(total[0:128], 1, 1))
    after = jnp.where(lane == 127, 0.0, pltpu.roll(total[256:384], 127, 1))
    return total[128:256] + (before + after)


def outer_kernel(pre, taps, halo, f0, f1, f2, f3, o0, o1, o2, o3):
    parts = jnp.concatenate([f[pl.ds(432, 16)].astype(F32) for f in (f0, f1, f2, f3)], axis=0)
    offset = (parts[:, 0:1] + parts[:, 1:2]) + parts[:, 2:3]
    offset = jnp.concatenate([offset, offset], axis=0)
    lane16 = lanes_of((16, 128))
    sides = []
    for side in range(2):
        depths = []
        for z in range(2):
            total = jnp.zeros((16, 128), F32)
            for src in range(8):
                piece = halo[src, pl.ds(64, 16)].astype(F32)
                shift = (src * 16 - (side * 32 + z * 16)) % 128
                piece = pltpu.roll(piece, shift, 1) if shift else piece
                total = jnp.where(lane16 // 16 == src, piece, total)
            depths.append(total)
        sides.append(jnp.concatenate(depths, axis=1))
    beside = jnp.concatenate(
        [jnp.concatenate([sides[0][b : b + 8], sides[1][b : b + 8]], axis=0) for b in range(3)], axis=1
    ).astype(BF)
    edge = lax.dot_general(
        taps[...], beside, (((1,), (1,)), ((), ())), preferred_element_type=F32
    )
    lane = lanes_of((128, 128))
    more = []
    for side in range(2):
        beyond = jnp.concatenate(
            [halo[src, pl.ds(side * 32 + z * 16, 16)] for z in range(2) for src in range(8)], axis=0
        )
        near = taps[:, pl.ds(side * 512, 256)]
        more.append(aligned(jnp.dot(near, beyond, preferred_element_type=F32), lane))
    for row in range(8):
        total = pre[row] + offset
        if row == 0:
            total = total + more[0]
        if row == 7:
            total = total + more[1]
        total = total + jnp.where(lane == 0, edge[0:128, row : row + 1], 0.0)
        total = total + jnp.where(lane == 127, edge[256:384, 8 + row : 9 + row], 0.0)
        done = jnp.where(total >= 0, total, 0.3 * total).astype(BF)
        for z in range(2):
            for t, out in enumerate((o0, o1, o2, o3)):
                out[z * 8 + row] = done[z * 64 + t * 16 : z * 64 + t * 16 + 16]


def unpack_kernel(g0, g1, g2, g3, out, flat):
    quarter = lax.rem(lax.axis_index("ch"), 4)
    for t, got in enumerate((g0, g1, g2, g3)):
        start = 8 * (quarter ^ t)
        for z in range(2):
            for r in range(8):
                flat[pl.ds(start + z * 32 + r, 16, stride=64), :] = got[z * 8 + r].astype(F32)
    out[...] = flat[...].reshape(16, 2, 32, 128).astype(BF)


def shifts(array, axis, up=True):
    size = lax.axis_size(axis)
    pairs = [(i, i + 1) for i in range(size - 1)]
    return lax.ppermute(array, axis, pairs if up else [(j, i) for i, j in pairs])


def thirds(bias):
    high = bias.astype(BF)
    rest = bias - high.astype(F32)
    middle = rest.astype(BF)
    low = (rest - middle.astype(F32)).astype(BF)
    return jnp.pad(jnp.stack([high, middle, low], axis=1), ((0, 0), (0, 125)))


def swapped(array, t):
    return lax.ppermute(array, "ch", [(d, d ^ t) for d in range(8)])


def stages(volume, weights, bias):
    slabs, first, last, edges = call(
        pack_kernel,
        [shaped(8, 16, 16, 128), shaped(32, 128), shaped(32, 128), shaped(4, 64, 128)],
        [pltpu.VMEM((1024, 128), F32)],
        volume,
        moved=1 << 20,
    )
    slabs = lax.all_to_all(slabs, "ch", split_axis=0, concat_axis=0, tiled=True)
    top = shifts(last, "sx", True)
    bottom = shifts(first, "sx", False)
    cols = call(columns_kernel, shaped(32, 128, dtype=F32), [], volume, moved=1 << 19)
    side = call(corner_kernel, shaped(40, 128), [pltpu.VMEM((40, 128), F32)], cols, top, bottom, moved=1 << 16)
    left = shifts(side, "sy", True)
    right = shifts(side, "sy", False)
    own = jnp.concatenate([weights.transpose(2, 3, 4, 0, 1).reshape(432, 128), thirds(bias)], axis=0)
    filters = (own,) + tuple(swapped(own, t) for t in (1, 2, 3))
    halo = call(halo_kernel, shaped(8, 80, 128), [], edges, top, bottom, left, right, moved=1 << 18)
    halo = lax.all_to_all(halo, "ch", split_axis=0, concat_axis=0, tiled=True)
    pre, taps = call(
        inner_kernel,
        [shaped(8, 128, 128, dtype=F32), shaped(384, 768)],
        [pltpu.VMEM((2048, 128), BF)],
        slabs,
        *filters,
        flops=2 * 384 * 768 * 1024,
        moved=3 << 20,
    )
    mine, *others = call(
        outer_kernel,
        [shaped(16, 16, 128)] * 4,
        [],
        pre,
        taps,
        halo,
        *filters,
        flops=2 * 384 * 768 * 128,
        moved=2 << 20,
    )
    others = [swapped(others[t - 1], t) for t in (1, 2, 3)]
    return call(
        unpack_kernel,
        shaped(16, 2, 32, 128),
        [pltpu.VMEM((1024, 128), F32)],
        mine,
        *others,
        moved=1 << 19,
    )


def solution(mesh):
    in_specs = (P("ch", None, "sx", "sy"), P("ch", None, None, None, None), P("ch"))
    out_specs = P("ch", None, "sx", "sy")
    return jax.shard_map(stages, mesh=mesh, in_specs=in_specs, out_specs=out_specs, check_vma=False)
```

```python
import jax
import jax.numpy as jnp
from jax import lax
from jax.experimental import pallas as pl
from jax.experimental.pallas import tpu as pltpu
from jax.sharding import PartitionSpec as P


BF = jnp.bfloat16
F32 = jnp.float32
GRANT = 16 << 20


def call(kernel, out_shapes, scratch, *args, flops=0, moved=0):
    vmem = pl.BlockSpec(memory_space=pltpu.VMEM)
    many = isinstance(out_shapes, (list, tuple))
    return pl.pallas_call(
        kernel,
        out_shape=out_shapes,
        in_specs=[vmem] * len(args),
        out_specs=[vmem] * len(out_shapes) if many else vmem,
        scratch_shapes=scratch,
        cost_estimate=pl.CostEstimate(flops=flops, bytes_accessed=moved, transcendentals=0),
        compiler_params=pltpu.CompilerParams(vmem_limit_bytes=GRANT),
    )(*args)


def shaped(*shape, dtype=BF):
    return jax.ShapeDtypeStruct(shape, dtype)


def lanes_of(shape):
    return lax.broadcasted_iota(jnp.int32, shape, len(shape) - 1)


def pack_kernel(vol, field, first, last, flat):
    flat[...] = vol[...].reshape(1024, 128).astype(F32)
    for z in range(2):
        for row in range(32):
            tile = flat[pl.ds(z * 32 + row, 16, stride=64), :].astype(BF)
            field[z * 32 + row] = tile
            if row == 0:
                first[pl.ds(z * 16, 16)] = tile
            if row == 31:
                last[pl.ds(z * 16, 16)] = tile


def columns_kernel(vol, cols):
    lane = lanes_of((32, 128))
    both = jnp.zeros((32, 128), F32)
    for z in range(2):
        for c in range(16):
            tile = vol[c, z].astype(F32)
            j = z * 16 + c
            both = jnp.where(lane == j, pltpu.roll(tile, j, 1) if j else tile, both)
            both = jnp.where(lane == 32 + j, pltpu.roll(tile, 33 + j, 1), both)
    cols[...] = both


def corner_kernel(cols, top, bottom, side, buf):
    both = jnp.concatenate(
        [top[...].astype(F32), bottom[...].astype(F32), jnp.zeros((64, 128), F32)], axis=0
    )
    turned = both.T
    first, last = turned[0:1, :], turned[127:128, :]
    lane = lanes_of((1, 128))
    buf[...] = jnp.zeros((40, 128), F32)
    buf[pl.ds(1, 32), :] = cols[...]
    buf[pl.ds(0, 1), :] = jnp.where(lane < 32, first, pltpu.roll(last, 32, 1))
    buf[pl.ds(33, 1), :] = jnp.where(lane < 32, pltpu.roll(first, 96, 1), last)
    side[...] = buf[...].astype(BF)


def halo_kernel(top, bottom, sides, out):
    me, size = lax.axis_index("sy"), lax.axis_size("sy")
    left = sides[jnp.maximum(me - 1, 0)].astype(F32)
    right = sides[jnp.minimum(me + 1, size - 1)].astype(F32)
    lane = lanes_of((40, 128))
    nothing = jnp.zeros((40, 128), F32)
    beside = jnp.where(
        lane < 32,
        jnp.where(me > 0, pltpu.roll(left, 96, 1), nothing),
        jnp.where(me < size - 1, pltpu.roll(right, 32, 1), nothing),
    )
    both = jnp.where(lanes_of((24, 128)) < 64, beside[0:24], pltpu.roll(beside[16:40], 64, 1)).astype(BF)
    for d in range(8):
        out[d, pl.ds(0, 32)] = top[...]
        out[d, pl.ds(32, 32)] = bottom[...]
        out[d, pl.ds(64, 24)] = both


def taps_kernel(own, taps):
    me = lax.axis_index("ch")
    chip, core = me // 2, lax.rem(me, 2)
    lane = lanes_of((16, 128))
    turned = []
    for tap in range(27):
        tile = pltpu.roll(own[pl.ds(tap * 16, 16)].astype(F32), lax.rem(128 - 32 * chip, 128), 1)
        other = jnp.where(lax.rem(lane // 16, 2) == 0, pltpu.roll(tile, 112, 1), pltpu.roll(tile, 16, 1))
        turned.append(jnp.where(core == 1, other, tile).astype(BF))
    for b in range(3):
        for e in range(3):
            for zo in range(2):
                for zi in range(2):
                    tile = turned[(zi - zo + 1) * 9 + b * 3 + e]
                    taps[pl.ds(((b * 3 + e) * 2 + zo) * 16, 16), pl.ds(zi * 128, 128)] = tile


def conv_kernel(p0, p1, p2, p3, p4, p5, p6, p7, halo, taps, bias, out, sums, flat):
    pieces = (p0, p1, p2, p3, p4, p5, p6, p7)
    me = lax.axis_index("ch")
    chip, core = me // 2, lax.rem(me, 2)
    sources = [2 * lax.rem(chip + j // 2, 4) + (core ^ (j % 2)) for j in range(8)]
    lane40 = lanes_of((40, 128))
    total = [[jnp.zeros((40, 128), F32) for _ in range(2)] for _ in range(2)]
    for j, source in enumerate(sources):
        both = halo[source, pl.ds(64, 24)].astype(F32)
        both = jnp.concatenate([both, pltpu.roll(both[8:24], 64, 1)], axis=0)
        for side in range(2):
            for z in range(2):
                shift = (j * 16 - side * 32 - z * 16) % 128
                piece = pltpu.roll(both, shift, 1) if shift else both
                total[side][z] = jnp.where(lane40 // 16 == j, piece, total[side][z])
    beside = jnp.concatenate(
        [jnp.concatenate(total[0], axis=1), jnp.concatenate(total[1], axis=1), jnp.zeros((48, 256), F32)], axis=0
    ).astype(BF)
    edge = lax.dot_general(taps[...], beside, (((1,), (1,)), ((), ())), preferred_element_type=F32)
    ends = [
        edge[e * 32 : e * 32 + 32]
        + pltpu.roll(edge[96 + e * 32 : 128 + e * 32], 127, 1)
        + pltpu.roll(edge[192 + e * 32 : 224 + e * 32], 126, 1)
        for e in (0, 2)
    ]
    offset = jnp.concatenate([bias[...], bias[...]], axis=0)
    lane = lanes_of((32, 128))

    def row_of(at):
        if at == 0 or at == 33:
            below = 32 if at else 0
            return jnp.concatenate(
                [halo[source, pl.ds(below + z * 16, 16)] for z in range(2) for source in sources], axis=0
            )
        return jnp.concatenate([piece[z * 32 + at - 1] for z in range(2) for piece in pieces], axis=0)

    for p in range(17):
        pair = jnp.concatenate([row_of(2 * p), row_of(2 * p + 1)], axis=1)
        got = jnp.dot(taps[...], pair, preferred_element_type=F32)
        for h in range(2):
            for b in range(3):
                row = 2 * p + h - b
                if not 0 <= row < 32:
                    continue
                part = got[b * 96 : (b + 1) * 96, h * 128 : (h + 1) * 128]
                if b == 0:
                    sums[row] = part
                    continue
                part = part + sums[row]
                if b == 1:
                    sums[row] = part
                    continue
                pre = part[32:64] + jnp.where(lane == 0, ends[0][:, row : row + 1], pltpu.roll(part[0:32], 1, 1))
                pre = pre + jnp.where(
                    lane == 127, ends[1][:, 40 + row : 41 + row], pltpu.roll(part[64:96], 127, 1)
                )
                pre = pre + offset
                pre = jnp.where(pre >= 0, pre, 0.3 * pre)
                for z in range(2):
                    flat[pl.ds(z * 32 + row, 16, stride=64), :] = pre[z * 16 : z * 16 + 16]
    out[...] = flat[...].reshape(16, 2, 32, 128).astype(BF)


def shifts(array, axis, up=True):
    size = lax.axis_size(axis)
    pairs = [(i, i + 1) for i in range(size - 1)]
    return lax.ppermute(array, axis, pairs if up else [(j, i) for i, j in pairs])


def cyclic(array, step):
    return lax.ppermute(array, "ch", [(d, (d + step) % 8) for d in range(8)])


def partner(array):
    return lax.ppermute(array, "ch", [(d, d ^ 1) for d in range(8)])


def stages(volume, weights, bias):
    field, first, last = call(
        pack_kernel,
        [shaped(64, 16, 128), shaped(32, 128), shaped(32, 128)],
        [pltpu.VMEM((1024, 128), F32)],
        volume,
        moved=1 << 20,
    )
    z4 = cyclic(field, 4)
    z2 = cyclic(field, 2)
    z6 = cyclic(field, 6)
    top = shifts(last, "sx", True)
    bottom = shifts(first, "sx", False)
    cols = call(columns_kernel, shaped(32, 128, dtype=F32), [], volume, moved=1 << 19)
    side = call(corner_kernel, shaped(40, 128), [pltpu.VMEM((40, 128), F32)], cols, top, bottom, moved=1 << 16)
    sides = lax.all_to_all(jnp.broadcast_to(side, (8, 40, 128)), "sy", split_axis=0, concat_axis=0, tiled=True)
    own = weights.transpose(2, 3, 4, 0, 1).reshape(432, 128)
    taps = call(taps_kernel, shaped(288, 256), [], own, moved=1 << 19)
    spread = jnp.broadcast_to(bias[:, None], (16, 128))
    halo = call(halo_kernel, shaped(8, 88, 128), [], top, bottom, sides, moved=1 << 18)
    halo = lax.all_to_all(halo, "ch", split_axis=0, concat_axis=0, tiled=True)
    f0 = partner(field)
    f4 = partner(z4)
    f2 = partner(z2)
    f6 = partner(z6)
    return call(
        conv_kernel,
        shaped(16, 2, 32, 128),
        [pltpu.VMEM((32, 96, 128), F32), pltpu.VMEM((1024, 128), F32)],
        field,
        f0,
        z6,
        f6,
        z4,
        f4,
        z2,
        f2,
        halo,
        taps,
        spread,
        flops=2 * 288 * 256 * 34 * 128,
        moved=3 << 20,
    )


def solution(mesh):
    in_specs = (P("ch", None, "sx", "sy"), P("ch", None, None, None, None), P("ch"))
    out_specs = P("ch", None, "sx", "sy")
    return jax.shard_map(stages, mesh=mesh, in_specs=in_specs, out_specs=out_specs, check_vma=False)
```

```python
import jax
import jax.numpy as jnp
from jax import lax
from jax.experimental import pallas as pl
from jax.experimental.pallas import tpu as pltpu
from jax.sharding import PartitionSpec as P


BF = jnp.bfloat16
F32 = jnp.float32
CORES = [[0, 2, 4, 6], [1, 3, 5, 7]]
GRANT = 16 << 20


def call(kernel, out_shapes, scratch, *args, flops=0, moved=0):
    vmem = pl.BlockSpec(memory_space=pltpu.VMEM)
    many = isinstance(out_shapes, (list, tuple))
    return pl.pallas_call(
        kernel,
        out_shape=out_shapes,
        in_specs=[vmem] * len(args),
        out_specs=[vmem] * len(out_shapes) if many else vmem,
        scratch_shapes=scratch,
        cost_estimate=pl.CostEstimate(flops=flops, bytes_accessed=moved, transcendentals=0),
        compiler_params=pltpu.CompilerParams(vmem_limit_bytes=GRANT),
    )(*args)


def shaped(*shape, dtype=BF):
    return jax.ShapeDtypeStruct(shape, dtype)


def lanes_of(shape):
    return lax.broadcasted_iota(jnp.int32, shape, len(shape) - 1)


def pack_kernel(vol, blocks, first, last, cols, flat):
    flat[...] = vol[...].reshape(1024, 128).astype(F32)
    for z in range(2):
        for row in range(32):
            tile = flat[pl.ds(z * 32 + row, 16, stride=64), :].astype(BF)
            for chip in range(4):
                at = row - 15 * (chip % 2)
                if 0 <= at < 17:
                    blocks[chip, z * 17 + at] = tile
            if row == 0:
                first[pl.ds(z * 16, 16)] = tile
            if row == 31:
                last[pl.ds(z * 16, 16)] = tile
    lane = lanes_of((32, 128))
    both = jnp.zeros((32, 128), F32)
    for z in range(2):
        for c in range(16):
            tile = flat[pl.ds(c * 64 + z * 32, 32), :]
            j = z * 16 + c
            both = jnp.where(lane == j, pltpu.roll(tile, j, 1) if j else tile, both)
            both = jnp.where(lane == 32 + j, pltpu.roll(tile, 33 + j, 1), both)
    cols[...] = both.astype(BF)


def beside_kernel(first, last, left, right, up, down, beside):
    lane = lanes_of((32, 128))
    both = jnp.where(
        lane < 32,
        pltpu.roll(left[...].astype(F32), 96, 1),
        jnp.where(lane < 64, pltpu.roll(right[...].astype(F32), 32, 1), 0.0),
    )
    beside[...] = both
    nothing = jnp.zeros((15, 128), F32)
    up[pl.ds(0, 32)] = last[...]
    up[pl.ds(32, 16)] = jnp.concatenate([both[31:32], nothing], axis=0).astype(BF)
    down[pl.ds(0, 32)] = first[...]
    down[pl.ds(32, 16)] = jnp.concatenate([both[0:1], nothing], axis=0).astype(BF)


def halo_kernel(above, below, beside, out, buf):
    buf[...] = jnp.zeros((40, 128), F32)
    buf[pl.ds(0, 1), :] = above[pl.ds(32, 16)].astype(F32)[0:1]
    buf[pl.ds(1, 32), :] = beside[...]
    buf[pl.ds(33, 1), :] = below[pl.ds(32, 16)].astype(F32)[0:1]
    for d in range(8):
        half = d // 2 % 2
        out[d, pl.ds(0, 32)] = below[pl.ds(0, 32)] if half else above[pl.ds(0, 32)]
        out[d, pl.ds(32, 24)] = buf[pl.ds(16 * half, 24), :].astype(BF)


def taps_kernel(own, other, taps):
    odd = lax.rem(lax.axis_index("ch"), 2) == 1
    even_block = lax.rem(lanes_of((16, 128)) // 16, 2) == 0
    for t, filters in enumerate((own, other)):
        for a in range(3):
            for b in range(3):
                for e in range(3):
                    tile = filters[pl.ds((a * 9 + b * 3 + e) * 16, 16)].astype(F32)
                    swapped = jnp.where(even_block, pltpu.roll(tile, 112, 1), pltpu.roll(tile, 16, 1))
                    tile = jnp.where(odd, swapped, tile).astype(BF)
                    for zo in range(2):
                        zi = a - 1 + zo
                        if 0 <= zi < 2:
                            taps[
                                pl.ds((((b * 3 + e) * 2 + zo) * 2 + t) * 16, 16), pl.ds(zi * 128, 128)
                            ] = tile


def aligned(total, lane):
    before = jnp.where(lane == 0, 0.0, pltpu.roll(total[0:64], 1, 1))
    after = jnp.where(lane == 127, 0.0, pltpu.roll(total[128:192], 127, 1))
    return total[64:128] + (before + after)


def inner_kernel(mine, theirs, taps, pre, sums):
    half = lax.rem(lax.axis_index("ch") // 2, 2)
    lane = lanes_of((64, 128))

    def row_of(row):
        return jnp.concatenate(
            [held[chip, z * 17 + row + half] for z in range(2) for chip in range(4) for held in (mine, theirs)],
            axis=0,
        )

    for p in range(8):
        pair = jnp.concatenate([row_of(2 * p), row_of(2 * p + 1)], axis=1)
        got = jnp.dot(taps[...], pair, preferred_element_type=F32)
        for h in range(2):
            for b in range(3):
                row = 2 * p + h + 1 - b
                if not 0 <= row < 16:
                    continue
                part = got[b * 192 : (b + 1) * 192, h * 128 : (h + 1) * 128]
                if not (b == 0 or (b == 1 and row == 0)):
                    part = part + sums[row]
                if b == 2 or (b == 1 and row == 15):
                    pre[row] = aligned(part, lane)
                else:
                    sums[row] = part


def outer_kernel(pre, taps, mine, theirs, halo, own, other, kept, sent):
    me = lax.axis_index("ch")
    half, core = lax.rem(me // 2, 2), lax.rem(me, 2)
    parts = jnp.concatenate([f[pl.ds(432, 16)].astype(F32) for f in (own, other)], axis=0)
    offset = (parts[:, 0:1] + parts[:, 1:2]) + parts[:, 2:3]
    offset = jnp.concatenate([offset, offset], axis=0)
    sources = [2 * chip + (core ^ t) for chip in range(4) for t in range(2)]
    lane24 = lanes_of((24, 128))
    total = [[jnp.zeros((24, 128), F32) for _ in range(2)] for _ in range(2)]
    for j, source in enumerate(sources):
        both = halo[source, pl.ds(32, 24)].astype(F32)
        for side in range(2):
            for z in range(2):
                shift = (j * 16 - side * 32 - z * 16) % 128
                piece = pltpu.roll(both, shift, 1) if shift else both
                total[side][z] = jnp.where(lane24 // 16 == j, piece, total[side][z])
    beside = jnp.concatenate(
        [jnp.concatenate(total[0], axis=1), jnp.concatenate(total[1], axis=1), jnp.zeros((80, 256), F32)], axis=0
    ).astype(BF)
    edge = lax.dot_general(taps[...], beside, (((1,), (1,)), ((), ())), preferred_element_type=F32)
    before, after = (
        edge[e * 64 : e * 64 + 64]
        + pltpu.roll(edge[192 + e * 64 : 256 + e * 64], 127, 1)
        + pltpu.roll(edge[384 + e * 64 : 448 + e * 64], 126, 1)
        for e in (0, 2)
    )
    lane = lanes_of((64, 128))
    ends = [
        jnp.concatenate(
            [halo[source, pl.ds(z * 16, 16)] for z in range(2) for source in sources], axis=0
        )
    ]
    ends.append(
        jnp.concatenate(
            [
                held[chip, z * 17 + 16 * (1 - half)]
                for z in range(2)
                for chip in range(4)
                for held in (mine, theirs)
            ],
            axis=0,
        )
    )
    first_half = half == 0
    above = jnp.where(first_half, ends[0].astype(F32), ends[1].astype(F32)).astype(BF)
    below = jnp.where(first_half, ends[1].astype(F32), ends[0].astype(F32)).astype(BF)
    above = aligned(jnp.dot(taps[pl.ds(0, 192)], above, preferred_element_type=F32), lane)
    below = aligned(jnp.dot(taps[pl.ds(384, 192)], below, preferred_element_type=F32), lane)
    for row in range(16):
        total = pre[row] + offset
        if row == 0:
            total = total + above
        if row == 15:
            total = total + below
        total = total + jnp.where(lane == 0, before[:, row : row + 1], 0.0)
        total = total + jnp.where(lane == 127, after[:, 24 + row : 25 + row], 0.0)
        done = jnp.where(total >= 0, total, 0.3 * total).astype(BF)
        for z in range(2):
            kept[z * 16 + row] = done[z * 32 : z * 32 + 16]
            sent[z * 16 + row] = done[z * 32 + 16 : z * 32 + 32]


def unpack_kernel(kept, got, out, flat):
    half = lax.rem(lax.axis_index("ch") // 2, 2)
    for held, start in ((kept, 16 * half), (got, 16 * (1 - half))):
        for z in range(2):
            for row in range(16):
                flat[pl.ds(start + z * 32 + row, 16, stride=64), :] = held[z * 16 + row].astype(F32)
    out[...] = flat[...].reshape(16, 2, 32, 128).astype(BF)


def shifts(array, axis, up=True):
    size = lax.axis_size(axis)
    pairs = [(i, i + 1) for i in range(size - 1)]
    return lax.ppermute(array, axis, pairs if up else [(j, i) for i, j in pairs])


def swapped(array, t):
    return lax.ppermute(array, "ch", [(d, d ^ t) for d in range(8)])


def thirds(bias):
    high = bias.astype(BF)
    rest = bias - high.astype(F32)
    middle = rest.astype(BF)
    low = (rest - middle.astype(F32)).astype(BF)
    return jnp.pad(jnp.stack([high, middle, low], axis=1), ((0, 0), (0, 125)))


def stages(volume, weights, bias):
    blocks, first, last, cols = call(
        pack_kernel,
        [shaped(4, 34, 16, 128), shaped(32, 128), shaped(32, 128), shaped(32, 128)],
        [pltpu.VMEM((1024, 128), F32)],
        volume,
        moved=1 << 20,
    )
    mine = lax.all_to_all(blocks, "ch", split_axis=0, concat_axis=0, tiled=True, axis_index_groups=CORES)
    left = shifts(cols, "sy", True)
    right = shifts(cols, "sy", False)
    own = jnp.concatenate([weights.transpose(2, 3, 4, 0, 1).reshape(432, 128), thirds(bias)], axis=0)
    other = swapped(own, 2)
    up, down, beside = call(
        beside_kernel,
        [shaped(48, 128), shaped(48, 128), shaped(32, 128, dtype=F32)],
        [],
        first,
        last,
        left,
        right,
        moved=1 << 16,
    )
    above = shifts(up, "sx", True)
    below = shifts(down, "sx", False)
    theirs = swapped(mine, 1)
    taps = call(taps_kernel, shaped(576, 256), [], own, other, moved=1 << 19)
    halo = call(halo_kernel, shaped(8, 56, 128), [pltpu.VMEM((40, 128), F32)], above, below, beside, moved=1 << 17)
    halo = lax.all_to_all(halo, "ch", split_axis=0, concat_axis=0, tiled=True)
    pre = call(
        inner_kernel,
        shaped(16, 64, 128, dtype=F32),
        [pltpu.VMEM((16, 192, 128), F32)],
        mine,
        theirs,
        taps,
        flops=2 * 576 * 256 * 2048,
        moved=3 << 20,
    )
    kept, sent = call(
        outer_kernel,
        [shaped(32, 16, 128)] * 2,
        [],
        pre,
        taps,
        mine,
        theirs,
        halo,
        own,
        other,
        flops=2 * 576 * 256 * 256,
        moved=2 << 20,
    )
    got = swapped(sent, 2)
    return call(
        unpack_kernel,
        shaped(16, 2, 32, 128),
        [pltpu.VMEM((1024, 128), F32)],
        kept,
        got,
        moved=1 << 19,
    )


def solution(mesh):
    in_specs = (P("ch", None, "sx", "sy"), P("ch", None, None, None, None), P("ch"))
    out_specs = P("ch", None, "sx", "sy")
    return jax.shard_map(stages, mesh=mesh, in_specs=in_specs, out_specs=out_specs, check_vma=False)
```

```python
import jax
import jax.numpy as jnp
from jax import lax
from jax.experimental import pallas as pl
from jax.experimental.pallas import tpu as pltpu
from jax.sharding import PartitionSpec as P


BF = jnp.bfloat16
F32 = jnp.float32
CORES = [[0, 2, 4, 6], [1, 3, 5, 7]]
GRANT = 16 << 20


def call(kernel, out_shapes, scratch, *args, flops=0, moved=0):
    vmem = pl.BlockSpec(memory_space=pltpu.VMEM)
    many = isinstance(out_shapes, (list, tuple))
    return pl.pallas_call(
        kernel,
        out_shape=out_shapes,
        in_specs=[vmem] * len(args),
        out_specs=[vmem] * len(out_shapes) if many else vmem,
        scratch_shapes=scratch,
        cost_estimate=pl.CostEstimate(flops=flops, bytes_accessed=moved, transcendentals=0),
        compiler_params=pltpu.CompilerParams(vmem_limit_bytes=GRANT),
    )(*args)


def shaped(*shape, dtype=BF):
    return jax.ShapeDtypeStruct(shape, dtype)


def lanes_of(shape):
    return lax.broadcasted_iota(jnp.int32, shape, len(shape) - 1)


def pack_kernel(vol, blocks, flat):
    flat[...] = vol[...].reshape(1024, 128).astype(F32)
    for z in range(2):
        for row in range(32):
            tile = flat[pl.ds(z * 32 + row, 16, stride=64), :].astype(BF)
            for chip in range(4):
                at = row - 15 * (chip % 2)
                if 0 <= at < 17:
                    blocks[chip, z * 17 + at] = tile


def half_of():
    return lax.rem(lax.axis_index("ch") // 2, 2)


def row_kernel(mine, row):
    at = 16 * half_of()
    for z in range(2):
        for chip in range(4):
            row[pl.ds(z * 64 + chip * 16, 16)] = mine[chip, z * 17 + at]


def columns_kernel(mine, cols):
    lane = lanes_of((128, 128))
    both = jnp.zeros((128, 128), F32)
    for i in range(17):
        tile = jnp.concatenate([mine[chip, z * 17 + i] for z in range(2) for chip in range(4)], axis=0).astype(F32)
        both = jnp.where(lane == i + 1, pltpu.roll(tile, i + 1, 1), both)
        both = jnp.where(lane == 65 + i, pltpu.roll(tile, 66 + i, 1), both)
    cols[...] = both


def edges_kernel(cols, beyond, edges):
    lane = lanes_of((128, 128))
    at = 18 * half_of()
    tile = beyond[...].astype(F32)
    both = cols[...]
    both = jnp.where(
        lane == at, jnp.broadcast_to(tile[:, 0:1], (128, 128)), both
    )
    both = jnp.where(lane == 64 + at, jnp.broadcast_to(tile[:, 127:128], (128, 128)), both)
    edges[...] = both.astype(BF)


def beside_kernel(beyond, left, right, halo):
    halo[pl.ds(0, 128)] = beyond[...]
    lane = lanes_of((128, 128))
    halo[pl.ds(128, 128)] = jnp.where(
        lane < 64, pltpu.roll(left[...].astype(F32), 64, 1), pltpu.roll(right[...].astype(F32), 64, 1)
    ).astype(BF)


def taps_kernel(own, other, taps):
    odd = lax.rem(lax.axis_index("ch"), 2) == 1
    even_block = lax.rem(lanes_of((16, 128)) // 16, 2) == 0
    for t, filters in enumerate((own, other)):
        for a in range(3):
            for b in range(3):
                for e in range(3):
                    tile = filters[pl.ds((a * 9 + b * 3 + e) * 16, 16)].astype(F32)
                    swapped = jnp.where(even_block, pltpu.roll(tile, 112, 1), pltpu.roll(tile, 16, 1))
                    tile = jnp.where(odd, swapped, tile).astype(BF)
                    for zo in range(2):
                        zi = a - 1 + zo
                        if 0 <= zi < 2:
                            taps[
                                pl.ds((((b * 3 + e) * 2 + zo) * 2 + t) * 16, 16), pl.ds(zi * 128, 128)
                            ] = tile


def aligned(total, lane):
    before = jnp.where(lane == 0, 0.0, pltpu.roll(total[0:64], 1, 1))
    after = jnp.where(lane == 127, 0.0, pltpu.roll(total[128:192], 127, 1))
    return total[64:128] + (before + after)


def inner_kernel(mine, theirs, taps, pre, sums):
    half = lax.rem(lax.axis_index("ch") // 2, 2)
    lane = lanes_of((64, 128))

    def row_of(row):
        return jnp.concatenate(
            [held[chip, z * 17 + row + half] for z in range(2) for chip in range(4) for held in (mine, theirs)],
            axis=0,
        )

    for p in range(8):
        pair = jnp.concatenate([row_of(2 * p), row_of(2 * p + 1)], axis=1)
        got = jnp.dot(taps[...], pair, preferred_element_type=F32)
        for h in range(2):
            for b in range(3):
                row = 2 * p + h + 1 - b
                if not 0 <= row < 16:
                    continue
                part = got[b * 192 : (b + 1) * 192, h * 128 : (h + 1) * 128]
                if not (b == 0 or (b == 1 and row == 0)):
                    part = part + sums[row]
                if b == 2 or (b == 1 and row == 15):
                    pre[row] = aligned(part, lane)
                else:
                    sums[row] = part


def outer_kernel(pre, taps, mine, theirs, halo, halo2, own, other, kept, sent):
    half = half_of()
    first_half = half == 0
    parts = jnp.concatenate([f[pl.ds(432, 16)].astype(F32) for f in (own, other)], axis=0)
    offset = (parts[:, 0:1] + parts[:, 1:2]) + parts[:, 2:3]
    offset = jnp.concatenate([offset, offset], axis=0)

    def joined(start):
        return jnp.concatenate(
            [
                held[pl.ds(start + z * 64 + chip * 16, 16)]
                for z in range(2)
                for chip in range(4)
                for held in (halo, halo2)
            ],
            axis=0,
        )

    edge = jnp.dot(taps[...], joined(128), preferred_element_type=F32)
    moved = []
    for e in (0, 2):
        total = (
            edge[e * 64 : e * 64 + 64]
            + pltpu.roll(edge[192 + e * 64 : 256 + e * 64], 127, 1)
            + pltpu.roll(edge[384 + e * 64 : 448 + e * 64], 126, 1)
        )
        moved.append(jnp.where(first_half, total, pltpu.roll(total, 127, 1)))
    before, after = moved
    lane = lanes_of((64, 128))
    far = joined(0).astype(F32)
    near = jnp.concatenate(
        [
            held[chip, z * 17 + 16 * (1 - half)]
            for z in range(2)
            for chip in range(4)
            for held in (mine, theirs)
        ],
        axis=0,
    ).astype(F32)
    above = jnp.where(first_half, far, near).astype(BF)
    below = jnp.where(first_half, near, far).astype(BF)
    above = aligned(jnp.dot(taps[pl.ds(0, 192)], above, preferred_element_type=F32), lane)
    below = aligned(jnp.dot(taps[pl.ds(384, 192)], below, preferred_element_type=F32), lane)
    for row in range(16):
        total = pre[row] + offset
        if row == 0:
            total = total + above
        if row == 15:
            total = total + below
        total = total + jnp.where(lane == 0, before[:, row : row + 1], 0.0)
        total = total + jnp.where(lane == 127, after[:, 64 + row : 65 + row], 0.0)
        done = jnp.where(total >= 0, total, 0.3 * total).astype(BF)
        for z in range(2):
            kept[z * 16 + row] = done[z * 32 : z * 32 + 16]
            sent[z * 16 + row] = done[z * 32 + 16 : z * 32 + 32]


def unpack_kernel(kept, got, out, flat):
    half = lax.rem(lax.axis_index("ch") // 2, 2)
    for held, start in ((kept, 16 * half), (got, 16 * (1 - half))):
        for z in range(2):
            for row in range(16):
                flat[pl.ds(start + z * 32 + row, 16, stride=64), :] = held[z * 16 + row].astype(F32)
    out[...] = flat[...].reshape(16, 2, 32, 128).astype(BF)


def along_y(array, step):
    size = lax.axis_size("sy")
    pairs = [
        (y * 8 + d, (y + step) * 8 + (d ^ 4)) for y in range(size) for d in range(8) if 0 <= y + step < size
    ]
    return lax.ppermute(array, ("sy", "ch"), pairs)


def along_x(array):
    size = lax.axis_size("sx")
    pairs = []
    for x in range(size):
        for d in range(8):
            to = x + (1 if d // 2 % 2 else -1)
            if 0 <= to < size:
                pairs.append((x * 8 + d, to * 8 + (d ^ 2)))
    return lax.ppermute(array, ("sx", "ch"), pairs)


def swapped(array, t):
    return lax.ppermute(array, "ch", [(d, d ^ t) for d in range(8)])


def thirds(bias):
    high = bias.astype(BF)
    rest = bias - high.astype(F32)
    middle = rest.astype(BF)
    low = (rest - middle.astype(F32)).astype(BF)
    return jnp.pad(jnp.stack([high, middle, low], axis=1), ((0, 0), (0, 125)))


def stages(volume, weights, bias):
    blocks = call(
        pack_kernel, shaped(4, 34, 16, 128), [pltpu.VMEM((1024, 128), F32)], volume, moved=1 << 20
    )
    mine = lax.all_to_all(blocks, "ch", split_axis=0, concat_axis=0, tiled=True, axis_index_groups=CORES)
    own = jnp.concatenate([weights.transpose(2, 3, 4, 0, 1).reshape(432, 128), thirds(bias)], axis=0)
    other = swapped(own, 2)
    row = call(row_kernel, shaped(128, 128), [], mine, moved=1 << 16)
    beyond = along_x(row)
    theirs = swapped(mine, 1)
    cols = call(columns_kernel, shaped(128, 128, dtype=F32), [], mine, moved=1 << 18)
    edges = call(edges_kernel, shaped(128, 128), [], cols, beyond, moved=1 << 17)
    left = along_y(edges, 1)
    right = along_y(edges, -1)
    taps = call(taps_kernel, shaped(576, 256), [], own, other, moved=1 << 19)
    pre = call(
        inner_kernel,
        shaped(16, 64, 128, dtype=F32),
        [pltpu.VMEM((16, 192, 128), F32)],
        mine,
        theirs,
        taps,
        flops=2 * 576 * 256 * 2048,
        moved=3 << 20,
    )
    halo = call(beside_kernel, shaped(256, 128), [], beyond, left, right, moved=1 << 17)
    halo2 = swapped(halo, 1)
    kept, sent = call(
        outer_kernel,
        [shaped(32, 16, 128)] * 2,
        [],
        pre,
        taps,
        mine,
        theirs,
        halo,
        halo2,
        own,
        other,
        flops=2 * 576 * 256 * 256,
        moved=2 << 20,
    )
    got = swapped(sent, 2)
    return call(
        unpack_kernel,
        shaped(16, 2, 32, 128),
        [pltpu.VMEM((1024, 128), F32)],
        kept,
        got,
        moved=1 << 19,
    )


def solution(mesh):
    in_specs = (P("ch", None, "sx", "sy"), P("ch", None, None, None, None), P("ch"))
    out_specs = P("ch", None, "sx", "sy")
    return jax.shard_map(stages, mesh=mesh, in_specs=in_specs, out_specs=out_specs, check_vma=False)
```

```python
import jax
import jax.numpy as jnp
from jax import lax
from jax.experimental import pallas as pl
from jax.experimental.pallas import tpu as pltpu
from jax.sharding import PartitionSpec as P


BF = jnp.bfloat16
F32 = jnp.float32
CORES = [[0, 2, 4, 6], [1, 3, 5, 7]]
GRANT = 20 << 20


def call(kernel, out_shapes, scratch, *args, flops=0, moved=0):
    vmem = pl.BlockSpec(memory_space=pltpu.VMEM)
    many = isinstance(out_shapes, (list, tuple))
    return pl.pallas_call(
        kernel,
        out_shape=out_shapes,
        in_specs=[vmem] * len(args),
        out_specs=[vmem] * len(out_shapes) if many else vmem,
        scratch_shapes=scratch,
        cost_estimate=pl.CostEstimate(flops=flops, bytes_accessed=moved, transcendentals=0),
        compiler_params=pltpu.CompilerParams(vmem_limit_bytes=GRANT),
    )(*args)


def shaped(*shape, dtype=BF):
    return jax.ShapeDtypeStruct(shape, dtype)


def lanes_of(shape):
    return lax.broadcasted_iota(jnp.int32, shape, len(shape) - 1)


def pack_kernel(vol, blocks, first, last, cols, flat):
    flat[...] = vol[...].reshape(1024, 128).astype(F32)
    for z in range(2):
        for row in range(32):
            tile = flat[pl.ds(z * 32 + row, 16, stride=64), :].astype(BF)
            for chip in range(4):
                blocks[chip, z * 32 + row] = tile
            if row == 0:
                first[pl.ds(z * 16, 16)] = tile
            if row == 31:
                last[pl.ds(z * 16, 16)] = tile
    lane = lanes_of((32, 128))
    both = jnp.zeros((32, 128), F32)
    for z in range(2):
        for c in range(16):
            tile = flat[pl.ds(c * 64 + z * 32, 32), :]
            j = z * 16 + c
            both = jnp.where(lane == j, pltpu.roll(tile, j, 1) if j else tile, both)
            both = jnp.where(lane == 32 + j, pltpu.roll(tile, 33 + j, 1), both)
    cols[...] = both.astype(BF)


def beside_kernel(first, last, left, right, up, down, beside):
    lane = lanes_of((32, 128))
    both = jnp.where(
        lane < 32,
        pltpu.roll(left[...].astype(F32), 96, 1),
        jnp.where(lane < 64, pltpu.roll(right[...].astype(F32), 32, 1), 0.0),
    )
    beside[...] = both
    nothing = jnp.zeros((15, 128), F32)
    up[pl.ds(0, 32)] = last[...]
    up[pl.ds(32, 16)] = jnp.concatenate([both[31:32], nothing], axis=0).astype(BF)
    down[pl.ds(0, 32)] = first[...]
    down[pl.ds(32, 16)] = jnp.concatenate([both[0:1], nothing], axis=0).astype(BF)


def halo_kernel(above, below, beside, out, buf):
    buf[...] = jnp.zeros((40, 128), F32)
    buf[pl.ds(0, 1), :] = above[pl.ds(32, 16)].astype(F32)[0:1]
    buf[pl.ds(1, 32), :] = beside[...]
    buf[pl.ds(33, 1), :] = below[pl.ds(32, 16)].astype(F32)[0:1]
    low, high = buf[pl.ds(0, 24), :], buf[pl.ds(16, 24), :]
    both = jnp.where(lanes_of((24, 128)) < 64, low, pltpu.roll(high, 64, 1)).astype(BF)
    for d in range(8):
        out[d, pl.ds(0, 32)] = above[pl.ds(0, 32)]
        out[d, pl.ds(32, 32)] = below[pl.ds(0, 32)]
        out[d, pl.ds(64, 24)] = both


def taps_kernel(own, taps):
    odd = lax.rem(lax.axis_index("ch"), 2) == 1
    even_block = lax.rem(lanes_of((16, 128)) // 16, 2) == 0
    for a in range(3):
        for b in range(3):
            for e in range(3):
                tile = own[pl.ds((a * 9 + b * 3 + e) * 16, 16)].astype(F32)
                swapped = jnp.where(even_block, pltpu.roll(tile, 112, 1), pltpu.roll(tile, 16, 1))
                tile = jnp.where(odd, swapped, tile).astype(BF)
                for zo in range(2):
                    zi = a - 1 + zo
                    if 0 <= zi < 2:
                        taps[pl.ds(((b * 3 + e) * 2 + zo) * 16, 16), pl.ds(zi * 128, 128)] = tile


def aligned(total, lane):
    before = jnp.where(lane == 0, 0.0, pltpu.roll(total[0:32], 1, 1))
    after = jnp.where(lane == 127, 0.0, pltpu.roll(total[64:96], 127, 1))
    return total[32:64] + (before + after)


def inner_kernel(mine, theirs, taps, pre, sums):
    lane = lanes_of((32, 128))

    def row_of(row):
        return jnp.concatenate(
            [held[chip, z * 32 + row] for z in range(2) for chip in range(4) for held in (mine, theirs)], axis=0
        )

    for p in range(16):
        pair = jnp.concatenate([row_of(2 * p), row_of(2 * p + 1)], axis=1)
        got = jnp.dot(taps[...], pair, preferred_element_type=F32)
        for h in range(2):
            for b in range(3):
                row = 2 * p + h + 1 - b
                if not 0 <= row < 32:
                    continue
                part = got[b * 96 : (b + 1) * 96, h * 128 : (h + 1) * 128]
                if not (b == 0 or (b == 1 and row == 0)):
                    part = part + sums[row]
                if b == 2 or (b == 1 and row == 31):
                    pre[row] = aligned(part, lane)
                else:
                    sums[row] = part


def outer_kernel(pre, taps, halo, bias, out, flat):
    core = lax.rem(lax.axis_index("ch"), 2)
    sources = [2 * chip + (core ^ t) for chip in range(4) for t in range(2)]
    lane40 = lanes_of((40, 128))
    total = [[jnp.zeros((40, 128), F32) for _ in range(2)] for _ in range(2)]
    for j, source in enumerate(sources):
        both = halo[source, pl.ds(64, 24)].astype(F32)
        both = jnp.concatenate([both, pltpu.roll(both[8:24], 64, 1)], axis=0)
        for side in range(2):
            for z in range(2):
                shift = (j * 16 - side * 32 - z * 16) % 128
                piece = pltpu.roll(both, shift, 1) if shift else both
                total[side][z] = jnp.where(lane40 // 16 == j, piece, total[side][z])
    beside = jnp.concatenate(
        [jnp.concatenate(total[0], axis=1), jnp.concatenate(total[1], axis=1), jnp.zeros((48, 256), F32)], axis=0
    ).astype(BF)
    edge = lax.dot_general(taps[...], beside, (((1,), (1,)), ((), ())), preferred_element_type=F32)
    before, after = (
        edge[e * 32 : e * 32 + 32]
        + pltpu.roll(edge[96 + e * 32 : 128 + e * 32], 127, 1)
        + pltpu.roll(edge[192 + e * 32 : 224 + e * 32], 126, 1)
        for e in (0, 2)
    )
    lane = lanes_of((32, 128))
    ends = []
    for side in range(2):
        beyond = jnp.concatenate(
            [halo[source, pl.ds(side * 32 + z * 16, 16)] for z in range(2) for source in sources], axis=0
        )
        near = taps[pl.ds(side * 192, 96)]
        ends.append(aligned(jnp.dot(near, beyond, preferred_element_type=F32), lane))
    offset = jnp.concatenate([bias[...], bias[...]], axis=0)
    for row in range(32):
        total = pre[row] + offset
        if row == 0:
            total = total + ends[0]
        if row == 31:
            total = total + ends[1]
        total = total + jnp.where(lane == 0, before[:, row : row + 1], 0.0)
        total = total + jnp.where(lane == 127, after[:, 40 + row : 41 + row], 0.0)
        total = jnp.where(total >= 0, total, 0.3 * total)
        for z in range(2):
            flat[pl.ds(z * 32 + row, 16, stride=64), :] = total[z * 16 : z * 16 + 16]
    out[...] = flat[...].reshape(16, 2, 32, 128).astype(BF)


def shifts(array, axis, up=True):
    size = lax.axis_size(axis)
    pairs = [(i, i + 1) for i in range(size - 1)]
    return lax.ppermute(array, axis, pairs if up else [(j, i) for i, j in pairs])


def swapped(array, t):
    return lax.ppermute(array, "ch", [(d, d ^ t) for d in range(8)])


def stages(volume, weights, bias):
    blocks, first, last, cols = call(
        pack_kernel,
        [shaped(4, 64, 16, 128), shaped(32, 128), shaped(32, 128), shaped(32, 128)],
        [pltpu.VMEM((1024, 128), F32)],
        volume,
        moved=1 << 20,
    )
    mine = lax.all_to_all(blocks, "ch", split_axis=0, concat_axis=0, tiled=True, axis_index_groups=CORES)
    left = shifts(cols, "sy", True)
    right = shifts(cols, "sy", False)
    own = weights.transpose(2, 3, 4, 0, 1).reshape(432, 128)
    taps = call(taps_kernel, shaped(288, 256), [], own, moved=1 << 19)
    spread = jnp.broadcast_to(bias[:, None], (16, 128))
    up, down, beside = call(
        beside_kernel,
        [shaped(48, 128), shaped(48, 128), shaped(32, 128, dtype=F32)],
        [],
        first,
        last,
        left,
        right,
        moved=1 << 16,
    )
    above = shifts(up, "sx", True)
    below = shifts(down, "sx", False)
    theirs = swapped(mine, 1)
    halo = call(halo_kernel, shaped(8, 88, 128), [pltpu.VMEM((40, 128), F32)], above, below, beside, moved=1 << 17)
    halo = lax.all_to_all(halo, "ch", split_axis=0, concat_axis=0, tiled=True)
    pre = call(
        inner_kernel,
        shaped(32, 32, 128, dtype=F32),
        [pltpu.VMEM((32, 96, 128), F32)],
        mine,
        theirs,
        taps,
        flops=2 * 288 * 256 * 4096,
        moved=3 << 20,
    )
    return call(
        outer_kernel,
        shaped(16, 2, 32, 128),
        [pltpu.VMEM((1024, 128), F32)],
        pre,
        taps,
        halo,
        spread,
        flops=2 * 288 * 256 * 256,
        moved=2 << 20,
    )


def solution(mesh):
    in_specs = (P("ch", None, "sx", "sy"), P("ch", None, None, None, None), P("ch"))
    out_specs = P("ch", None, "sx", "sy")
    return jax.shard_map(stages, mesh=mesh, in_specs=in_specs, out_specs=out_specs, check_vma=False)
```

```python
import jax
import jax.numpy as jnp
from jax import lax
from jax.experimental import pallas as pl
from jax.experimental.pallas import tpu as pltpu
from jax.sharding import PartitionSpec as P


BF = jnp.bfloat16
F32 = jnp.float32
CORES = [[0, 2, 4, 6], [1, 3, 5, 7]]
GRANT = 16 << 20


def call(kernel, out_shapes, scratch, *args, flops=0, moved=0):
    vmem = pl.BlockSpec(memory_space=pltpu.VMEM)
    many = isinstance(out_shapes, (list, tuple))
    return pl.pallas_call(
        kernel,
        out_shape=out_shapes,
        in_specs=[vmem] * len(args),
        out_specs=[vmem] * len(out_shapes) if many else vmem,
        scratch_shapes=scratch,
        cost_estimate=pl.CostEstimate(flops=flops, bytes_accessed=moved, transcendentals=0),
        compiler_params=pltpu.CompilerParams(vmem_limit_bytes=GRANT),
    )(*args)


def shaped(*shape, dtype=BF):
    return jax.ShapeDtypeStruct(shape, dtype)


def lanes_of(shape):
    return lax.broadcasted_iota(jnp.int32, shape, len(shape) - 1)


def pack_kernel(vol, blocks, first, last, cols, flat):
    flat[...] = vol[...].reshape(1024, 128).astype(F32)
    for z in range(2):
        for row in range(32):
            tile = flat[pl.ds(z * 32 + row, 16, stride=64), :].astype(BF)
            for chip in range(4):
                at = row - 15 * (chip % 2)
                if 0 <= at < 17:
                    blocks[chip, z * 17 + at] = tile
            if row == 0:
                first[pl.ds(z * 16, 16)] = tile
            if row == 31:
                last[pl.ds(z * 16, 16)] = tile
    lane = lanes_of((32, 128))
    both = jnp.zeros((32, 128), F32)
    for z in range(2):
        for c in range(16):
            tile = flat[pl.ds(c * 64 + z * 32, 32), :]
            j = z * 16 + c
            both = jnp.where(lane == j, pltpu.roll(tile, j, 1) if j else tile, both)
            both = jnp.where(lane == 32 + j, pltpu.roll(tile, 33 + j, 1), both)
    cols[...] = both.astype(BF)


def corner_kernel(cols, top, bottom, side, buf):
    both = jnp.concatenate(
        [top[...].astype(F32), bottom[...].astype(F32), jnp.zeros((64, 128), F32)], axis=0
    )
    turned = both.T
    first, last = turned[0:1, :], turned[127:128, :]
    lane = lanes_of((1, 128))
    buf[...] = jnp.zeros((40, 128), F32)
    buf[pl.ds(1, 32), :] = cols[...].astype(F32)
    buf[pl.ds(0, 1), :] = jnp.where(lane < 32, first, pltpu.roll(last, 32, 1))
    buf[pl.ds(33, 1), :] = jnp.where(lane < 32, pltpu.roll(first, 96, 1), last)
    side[...] = buf[...].astype(BF)


def halo_kernel(top, bottom, left, right, out):
    lane = lanes_of((40, 128))
    both = jnp.where(
        lane < 32, pltpu.roll(left[...].astype(F32), 96, 1), pltpu.roll(right[...].astype(F32), 32, 1)
    )
    for d in range(8):
        half = d // 2 % 2
        out[d, pl.ds(0, 32)] = bottom[...] if half else top[...]
        out[d, pl.ds(32, 24)] = both[16 * half : 16 * half + 24].astype(BF)


def taps_kernel(own, other, taps):
    odd = lax.rem(lax.axis_index("ch"), 2) == 1
    even_block = lax.rem(lanes_of((16, 128)) // 16, 2) == 0
    for t, filters in enumerate((own, other)):
        for a in range(3):
            for b in range(3):
                for e in range(3):
                    tile = filters[pl.ds((a * 9 + b * 3 + e) * 16, 16)].astype(F32)
                    swapped = jnp.where(even_block, pltpu.roll(tile, 112, 1), pltpu.roll(tile, 16, 1))
                    tile = jnp.where(odd, swapped, tile).astype(BF)
                    for zo in range(2):
                        zi = a - 1 + zo
                        if 0 <= zi < 2:
                            taps[
                                pl.ds((((b * 3 + e) * 2 + zo) * 2 + t) * 16, 16), pl.ds(zi * 128, 128)
                            ] = tile


def aligned(total, lane):
    before = jnp.where(lane == 0, 0.0, pltpu.roll(total[0:64], 1, 1))
    after = jnp.where(lane == 127, 0.0, pltpu.roll(total[128:192], 127, 1))
    return total[64:128] + (before + after)


def inner_kernel(mine, theirs, taps, pre, sums):
    half = lax.rem(lax.axis_index("ch") // 2, 2)
    lane = lanes_of((64, 128))

    def row_of(row):
        return jnp.concatenate(
            [held[chip, z * 17 + row + half] for z in range(2) for chip in range(4) for held in (mine, theirs)],
            axis=0,
        )

    for p in range(8):
        pair = jnp.concatenate([row_of(2 * p), row_of(2 * p + 1)], axis=1)
        got = jnp.dot(taps[...], pair, preferred_element_type=F32)
        for h in range(2):
            for b in range(3):
                row = 2 * p + h + 1 - b
                if not 0 <= row < 16:
                    continue
                part = got[b * 192 : (b + 1) * 192, h * 128 : (h + 1) * 128]
                if not (b == 0 or (b == 1 and row == 0)):
                    part = part + sums[row]
                if b == 2 or (b == 1 and row == 15):
                    pre[row] = aligned(part, lane)
                else:
                    sums[row] = part


def outer_kernel(pre, taps, mine, theirs, halo, own, other, kept, sent):
    me = lax.axis_index("ch")
    half, core = lax.rem(me // 2, 2), lax.rem(me, 2)
    parts = jnp.concatenate([f[pl.ds(432, 16)].astype(F32) for f in (own, other)], axis=0)
    offset = (parts[:, 0:1] + parts[:, 1:2]) + parts[:, 2:3]
    offset = jnp.concatenate([offset, offset], axis=0)
    sources = [2 * chip + (core ^ t) for chip in range(4) for t in range(2)]
    lane24 = lanes_of((24, 128))
    total = [[jnp.zeros((24, 128), F32) for _ in range(2)] for _ in range(2)]
    for j, source in enumerate(sources):
        both = halo[source, pl.ds(32, 24)].astype(F32)
        for side in range(2):
            for z in range(2):
                shift = (j * 16 - side * 32 - z * 16) % 128
                piece = pltpu.roll(both, shift, 1) if shift else both
                total[side][z] = jnp.where(lane24 // 16 == j, piece, total[side][z])
    beside = jnp.concatenate(
        [jnp.concatenate(total[0], axis=1), jnp.concatenate(total[1], axis=1), jnp.zeros((80, 256), F32)], axis=0
    ).astype(BF)
    edge = lax.dot_general(taps[...], beside, (((1,), (1,)), ((), ())), preferred_element_type=F32)
    before, after = (
        edge[e * 64 : e * 64 + 64]
        + pltpu.roll(edge[192 + e * 64 : 256 + e * 64], 127, 1)
        + pltpu.roll(edge[384 + e * 64 : 448 + e * 64], 126, 1)
        for e in (0, 2)
    )
    lane = lanes_of((64, 128))
    ends = [
        jnp.concatenate(
            [halo[source, pl.ds(z * 16, 16)] for z in range(2) for source in sources], axis=0
        )
    ]
    ends.append(
        jnp.concatenate(
            [
                held[chip, z * 17 + 16 * (1 - half)]
                for z in range(2)
                for chip in range(4)
                for held in (mine, theirs)
            ],
            axis=0,
        )
    )
    first_half = half == 0
    above = jnp.where(first_half, ends[0].astype(F32), ends[1].astype(F32)).astype(BF)
    below = jnp.where(first_half, ends[1].astype(F32), ends[0].astype(F32)).astype(BF)
    above = aligned(jnp.dot(taps[pl.ds(0, 192)], above, preferred_element_type=F32), lane)
    below = aligned(jnp.dot(taps[pl.ds(384, 192)], below, preferred_element_type=F32), lane)
    for row in range(16):
        total = pre[row] + offset
        if row == 0:
            total = total + above
        if row == 15:
            total = total + below
        total = total + jnp.where(lane == 0, before[:, row : row + 1], 0.0)
        total = total + jnp.where(lane == 127, after[:, 24 + row : 25 + row], 0.0)
        done = jnp.where(total >= 0, total, 0.3 * total).astype(BF)
        for z in range(2):
            kept[z * 16 + row] = done[z * 32 : z * 32 + 16]
            sent[z * 16 + row] = done[z * 32 + 16 : z * 32 + 32]


def unpack_kernel(kept, got, out, flat):
    half = lax.rem(lax.axis_index("ch") // 2, 2)
    for held, start in ((kept, 16 * half), (got, 16 * (1 - half))):
        for z in range(2):
            for row in range(16):
                flat[pl.ds(start + z * 32 + row, 16, stride=64), :] = held[z * 16 + row].astype(F32)
    out[...] = flat[...].reshape(16, 2, 32, 128).astype(BF)


def shifts(array, axis, up=True):
    size = lax.axis_size(axis)
    pairs = [(i, i + 1) for i in range(size - 1)]
    return lax.ppermute(array, axis, pairs if up else [(j, i) for i, j in pairs])


def swapped(array, t):
    return lax.ppermute(array, "ch", [(d, d ^ t) for d in range(8)])


def thirds(bias):
    high = bias.astype(BF)
    rest = bias - high.astype(F32)
    middle = rest.astype(BF)
    low = (rest - middle.astype(F32)).astype(BF)
    return jnp.pad(jnp.stack([high, middle, low], axis=1), ((0, 0), (0, 125)))


def stages(volume, weights, bias):
    blocks, first, last, cols = call(
        pack_kernel,
        [shaped(4, 34, 16, 128), shaped(32, 128), shaped(32, 128), shaped(32, 128)],
        [pltpu.VMEM((1024, 128), F32)],
        volume,
        moved=1 << 20,
    )
    mine = lax.all_to_all(blocks, "ch", split_axis=0, concat_axis=0, tiled=True, axis_index_groups=CORES)
    top = shifts(last, "sx", True)
    bottom = shifts(first, "sx", False)
    own = jnp.concatenate([weights.transpose(2, 3, 4, 0, 1).reshape(432, 128), thirds(bias)], axis=0)
    other = swapped(own, 2)
    side = call(corner_kernel, shaped(40, 128), [pltpu.VMEM((40, 128), F32)], cols, top, bottom, moved=1 << 16)
    left = shifts(side, "sy", True)
    right = shifts(side, "sy", False)
    theirs = swapped(mine, 1)
    taps = call(taps_kernel, shaped(576, 256), [], own, other, moved=1 << 19)
    halo = call(halo_kernel, shaped(8, 56, 128), [], top, bottom, left, right, moved=1 << 17)
    halo = lax.all_to_all(halo, "ch", split_axis=0, concat_axis=0, tiled=True)
    pre = call(
        inner_kernel,
        shaped(16, 64, 128, dtype=F32),
        [pltpu.VMEM((16, 192, 128), F32)],
        mine,
        theirs,
        taps,
        flops=2 * 576 * 256 * 2048,
        moved=3 << 20,
    )
    kept, sent = call(
        outer_kernel,
        [shaped(32, 16, 128)] * 2,
        [],
        pre,
        taps,
        mine,
        theirs,
        halo,
        own,
        other,
        flops=2 * 576 * 256 * 256,
        moved=2 << 20,
    )
    got = swapped(sent, 2)
    return call(
        unpack_kernel,
        shaped(16, 2, 32, 128),
        [pltpu.VMEM((1024, 128), F32)],
        kept,
        got,
        moved=1 << 19,
    )


def solution(mesh):
    in_specs = (P("ch", None, "sx", "sy"), P("ch", None, None, None, None), P("ch"))
    out_specs = P("ch", None, "sx", "sy")
    return jax.shard_map(stages, mesh=mesh, in_specs=in_specs, out_specs=out_specs, check_vma=False)
```

```python
import jax
import jax.numpy as jnp
from jax import lax
from jax.experimental import pallas as pl
from jax.experimental.pallas import tpu as pltpu
from jax.sharding import PartitionSpec as P


BF = jnp.bfloat16
F32 = jnp.float32
CORES = [[0, 2, 4, 6], [1, 3, 5, 7]]
GRANT = 16 << 20


def call(kernel, out_shapes, scratch, *args, flops=0, moved=0, place=None, shared=None):
    vmem = pl.BlockSpec(memory_space=pltpu.VMEM)
    many = isinstance(out_shapes, (list, tuple))
    in_specs = [vmem] * len(args)
    for i in shared or {}:
        in_specs[i] = pl.BlockSpec(memory_space=pl.ANY)
    return pl.pallas_call(
        kernel,
        out_shape=out_shapes,
        in_specs=in_specs,
        out_specs=[vmem] * len(out_shapes) if many else place or vmem,
        scratch_shapes=scratch,
        input_output_aliases=shared or {},
        cost_estimate=pl.CostEstimate(flops=flops, bytes_accessed=moved, transcendentals=0),
        compiler_params=pltpu.CompilerParams(vmem_limit_bytes=GRANT),
    )(*args)


def shaped(*shape, dtype=BF):
    return jax.ShapeDtypeStruct(shape, dtype)


def lanes_of(shape):
    return lax.broadcasted_iota(jnp.int32, shape, len(shape) - 1)


def columns_kernel(vol, cols):
    lane = lanes_of((32, 128))
    both = jnp.zeros((32, 128), F32)
    for z in range(2):
        for c in range(16):
            tile = vol[c, z].astype(F32)
            j = z * 16 + c
            both = jnp.where(lane == j, pltpu.roll(tile, j, 1) if j else tile, both)
            both = jnp.where(lane == 32 + j, pltpu.roll(tile, 33 + j, 1), both)
    cols[...] = both.astype(BF)


def pack_kernel(vol, blocks, first, last, flat):
    flat[...] = vol[...].reshape(1024, 128).astype(F32)
    for z in range(2):
        for row in range(32):
            tile = flat[pl.ds(z * 32 + row, 16, stride=64), :].astype(BF)
            for chip in range(4):
                at = row - 15 * (chip % 2)
                if 0 <= at < 17:
                    blocks[chip, z * 17 + at] = tile
            if row == 0:
                first[pl.ds(z * 16, 16)] = tile
            if row == 31:
                last[pl.ds(z * 16, 16)] = tile


def beside_kernel(first, last, left, right, up, down, beside):
    lane = lanes_of((32, 128))
    both = jnp.where(
        lane < 32,
        pltpu.roll(left[...].astype(F32), 96, 1),
        jnp.where(lane < 64, pltpu.roll(right[...].astype(F32), 32, 1), 0.0),
    )
    beside[...] = both
    nothing = jnp.zeros((15, 128), F32)
    up[pl.ds(0, 32)] = last[...]
    up[pl.ds(32, 16)] = jnp.concatenate([both[31:32], nothing], axis=0).astype(BF)
    down[pl.ds(0, 32)] = first[...]
    down[pl.ds(32, 16)] = jnp.concatenate([both[0:1], nothing], axis=0).astype(BF)


def halo_kernel(above, below, beside, out, buf):
    buf[...] = jnp.zeros((40, 128), F32)
    buf[pl.ds(0, 1), :] = above[pl.ds(32, 16)].astype(F32)[0:1]
    buf[pl.ds(1, 32), :] = beside[...]
    buf[pl.ds(33, 1), :] = below[pl.ds(32, 16)].astype(F32)[0:1]
    for d in range(8):
        half = d // 2 % 2
        out[d, pl.ds(0, 32)] = below[pl.ds(0, 32)] if half else above[pl.ds(0, 32)]
        out[d, pl.ds(32, 24)] = buf[pl.ds(16 * half, 24), :].astype(BF)


def taps_kernel(own, other, taps, taps2):
    odd = lax.rem(lax.axis_index("ch"), 2) == 1
    even_block = lax.rem(lanes_of((16, 128)) // 16, 2) == 0
    for filters, to in ((own, taps), (other, taps2)):
        for a in range(3):
            for b in range(3):
                for e in range(3):
                    tile = filters[pl.ds((a * 9 + b * 3 + e) * 16, 16)].astype(F32)
                    swapped = jnp.where(even_block, pltpu.roll(tile, 112, 1), pltpu.roll(tile, 16, 1))
                    tile = jnp.where(odd, swapped, tile).astype(BF)
                    for zo in range(2):
                        zi = a - 1 + zo
                        if 0 <= zi < 2:
                            to[pl.ds(((b * 3 + e) * 2 + zo) * 16, 16), pl.ds(zi * 128, 128)] = tile


def half_of():
    return lax.rem(lax.axis_index("ch") // 2, 2)


def aligned(total, lane):
    before = jnp.where(lane == 0, 0.0, pltpu.roll(total[0:32], 1, 1))
    after = jnp.where(lane == 127, 0.0, pltpu.roll(total[64:96], 127, 1))
    return total[32:64] + (before + after)


def inner_kernel(mine, theirs, taps, taps2, pre, pre2, sums):
    half = half_of()
    lane = lanes_of((32, 128))

    def row_of(row):
        return jnp.concatenate(
            [held[chip, z * 17 + row + half] for z in range(2) for chip in range(4) for held in (mine, theirs)],
            axis=0,
        )

    for p in range(8):
        pair = jnp.concatenate([row_of(2 * p), row_of(2 * p + 1)], axis=1)
        for t, (weights, to) in enumerate(((taps, pre), (taps2, pre2))):
            got = jnp.dot(weights[...], pair, preferred_element_type=F32)
            for h in range(2):
                for b in range(3):
                    row = 2 * p + h + 1 - b
                    if not 0 <= row < 16:
                        continue
                    part = got[b * 96 : (b + 1) * 96, h * 128 : (h + 1) * 128]
                    if not (b == 0 or (b == 1 and row == 0)):
                        part = part + sums[t, row]
                    if b == 2 or (b == 1 and row == 15):
                        to[row] = aligned(part, lane)
                    else:
                        sums[t, row] = part


def outer_kernel(pre, taps, mine, theirs, halo, filters, out):
    me = lax.axis_index("ch")
    half, core = half_of(), lax.rem(me, 2)
    parts = filters[pl.ds(432, 16)].astype(F32)
    offset = (parts[:, 0:1] + parts[:, 1:2]) + parts[:, 2:3]
    offset = jnp.concatenate([offset, offset], axis=0)
    sources = [2 * chip + (core ^ t) for chip in range(4) for t in range(2)]
    lane24 = lanes_of((24, 128))
    total = [[jnp.zeros((24, 128), F32) for _ in range(2)] for _ in range(2)]
    for j, source in enumerate(sources):
        both = halo[source, pl.ds(32, 24)].astype(F32)
        for side in range(2):
            for z in range(2):
                shift = (j * 16 - side * 32 - z * 16) % 128
                piece = pltpu.roll(both, shift, 1) if shift else both
                total[side][z] = jnp.where(lane24 // 16 == j, piece, total[side][z])
    beside = jnp.concatenate(
        [jnp.concatenate(total[0], axis=1), jnp.concatenate(total[1], axis=1), jnp.zeros((80, 256), F32)], axis=0
    ).astype(BF)
    edge = lax.dot_general(taps[...], beside, (((1,), (1,)), ((), ())), preferred_element_type=F32)
    before, after = (
        edge[e * 32 : e * 32 + 32]
        + pltpu.roll(edge[96 + e * 32 : 128 + e * 32], 127, 1)
        + pltpu.roll(edge[192 + e * 32 : 224 + e * 32], 126, 1)
        for e in (0, 2)
    )
    lane = lanes_of((32, 128))
    far = jnp.concatenate(
        [halo[source, pl.ds(z * 16, 16)] for z in range(2) for source in sources], axis=0
    ).astype(F32)
    near = jnp.concatenate(
        [
            held[chip, z * 17 + 16 * (1 - half)]
            for z in range(2)
            for chip in range(4)
            for held in (mine, theirs)
        ],
        axis=0,
    ).astype(F32)
    first_half = half == 0
    above = jnp.where(first_half, far, near).astype(BF)
    below = jnp.where(first_half, near, far).astype(BF)
    above = aligned(jnp.dot(taps[pl.ds(0, 96)], above, preferred_element_type=F32), lane)
    below = aligned(jnp.dot(taps[pl.ds(192, 96)], below, preferred_element_type=F32), lane)
    for row in range(16):
        total = pre[row] + offset
        if row == 0:
            total = total + above
        if row == 15:
            total = total + below
        total = total + jnp.where(lane == 0, before[:, row : row + 1], 0.0)
        total = total + jnp.where(lane == 127, after[:, 24 + row : 25 + row], 0.0)
        done = jnp.where(total >= 0, total, 0.3 * total).astype(BF)
        for z in range(2):
            out[z * 16 + row] = done[z * 16 : z * 16 + 16]


def store(held, out, start, flat, ready, sem):
    for z in range(2):
        for row in range(16):
            flat[pl.ds(z * 16 + row, 16, stride=32), :] = held[z * 16 + row].astype(F32)
    ready[...] = flat[...].reshape(16, 2, 16, 128).astype(BF)
    copy = pltpu.make_async_copy(ready, out.at[:, :, pl.ds(pl.multiple_of(start, 16), 16)], sem)
    copy.start()
    copy.wait()


def keep_kernel(kept, out, flat, ready, sem):
    store(kept, out, 16 * half_of(), flat, ready, sem)


def unpack_kernel(got, held, out, flat, ready, sem):
    store(got, out, 16 * (1 - half_of()), flat, ready, sem)


def shifts(array, axis, up=True):
    size = lax.axis_size(axis)
    pairs = [(i, i + 1) for i in range(size - 1)]
    return lax.ppermute(array, axis, pairs if up else [(j, i) for i, j in pairs])


def swapped(array, t):
    return lax.ppermute(array, "ch", [(d, d ^ t) for d in range(8)])


def thirds(bias):
    high = bias.astype(BF)
    rest = bias - high.astype(F32)
    middle = rest.astype(BF)
    low = (rest - middle.astype(F32)).astype(BF)
    return jnp.pad(jnp.stack([high, middle, low], axis=1), ((0, 0), (0, 125)))


def stages(volume, weights, bias):
    cols = call(columns_kernel, shaped(32, 128), [], volume, moved=1 << 19)
    blocks, first, last = call(
        pack_kernel,
        [shaped(4, 34, 16, 128), shaped(32, 128), shaped(32, 128)],
        [pltpu.VMEM((1024, 128), F32)],
        volume,
        moved=1 << 20,
    )
    mine = lax.all_to_all(blocks, "ch", split_axis=0, concat_axis=0, tiled=True, axis_index_groups=CORES)
    left = shifts(cols, "sy", True)
    right = shifts(cols, "sy", False)
    own = jnp.concatenate([weights.transpose(2, 3, 4, 0, 1).reshape(432, 128), thirds(bias)], axis=0)
    other = swapped(own, 2)
    up, down, beside = call(
        beside_kernel,
        [shaped(48, 128), shaped(48, 128), shaped(32, 128, dtype=F32)],
        [],
        first,
        last,
        left,
        right,
        moved=1 << 16,
    )
    above = shifts(up, "sx", True)
    below = shifts(down, "sx", False)
    theirs = swapped(mine, 1)
    taps, taps2 = call(taps_kernel, [shaped(288, 256)] * 2, [], own, other, moved=1 << 19)
    halo = call(halo_kernel, shaped(8, 56, 128), [pltpu.VMEM((40, 128), F32)], above, below, beside, moved=1 << 17)
    halo = lax.all_to_all(halo, "ch", split_axis=0, concat_axis=0, tiled=True)
    pre, pre2 = call(
        inner_kernel,
        [shaped(16, 32, 128, dtype=F32)] * 2,
        [pltpu.VMEM((2, 16, 96, 128), F32)],
        mine,
        theirs,
        taps,
        taps2,
        flops=2 * 576 * 256 * 2048,
        moved=3 << 20,
    )
    cost = dict(flops=2 * 288 * 256 * 256, moved=1 << 20)
    sent = call(outer_kernel, shaped(32, 16, 128), [], pre2, taps2, mine, theirs, halo, other, **cost)
    got = swapped(sent, 2)
    kept = call(outer_kernel, shaped(32, 16, 128), [], pre, taps, mine, theirs, halo, own, **cost)
    scratch = [pltpu.VMEM((512, 128), F32), pltpu.VMEM((16, 2, 16, 128), BF), pltpu.SemaphoreType.DMA]
    space = pl.BlockSpec(memory_space=pl.ANY)
    result = call(keep_kernel, shaped(16, 2, 32, 128), scratch, kept, moved=1 << 18, place=space)
    return call(unpack_kernel, shaped(16, 2, 32, 128), scratch, got, result, moved=1 << 18, place=space, shared={1: 0})


def solution(mesh):
    in_specs = (P("ch", None, "sx", "sy"), P("ch", None, None, None, None), P("ch"))
    out_specs = P("ch", None, "sx", "sy")
    return jax.shard_map(stages, mesh=mesh, in_specs=in_specs, out_specs=out_specs, check_vma=False)
```

```python
import jax
import jax.numpy as jnp
from jax import lax
from jax.experimental import pallas as pl
from jax.experimental.pallas import tpu as pltpu
from jax.sharding import PartitionSpec as P


BF = jnp.bfloat16
F32 = jnp.float32
CORES = [[0, 2, 4, 6], [1, 3, 5, 7]]
GRANT = 16 << 20


def call(kernel, out_shapes, scratch, *args, flops=0, moved=0, place=None, shared=None):
    vmem = pl.BlockSpec(memory_space=pltpu.VMEM)
    many = isinstance(out_shapes, (list, tuple))
    in_specs = [vmem] * len(args)
    for i in shared or {}:
        in_specs[i] = pl.BlockSpec(memory_space=pl.ANY)
    return pl.pallas_call(
        kernel,
        out_shape=out_shapes,
        in_specs=in_specs,
        out_specs=[vmem] * len(out_shapes) if many else place or vmem,
        scratch_shapes=scratch,
        input_output_aliases=shared or {},
        cost_estimate=pl.CostEstimate(flops=flops, bytes_accessed=moved, transcendentals=0),
        compiler_params=pltpu.CompilerParams(vmem_limit_bytes=GRANT),
    )(*args)


def shaped(*shape, dtype=BF):
    return jax.ShapeDtypeStruct(shape, dtype)


def lanes_of(shape):
    return lax.broadcasted_iota(jnp.int32, shape, len(shape) - 1)


def columns_kernel(vol, cols):
    lane = lanes_of((32, 128))
    both = jnp.zeros((32, 128), F32)
    for z in range(2):
        for c in range(16):
            tile = vol[c, z].astype(F32)
            j = z * 16 + c
            both = jnp.where(lane == j, pltpu.roll(tile, j, 1) if j else tile, both)
            both = jnp.where(lane == 32 + j, pltpu.roll(tile, 33 + j, 1), both)
    cols[...] = both.astype(BF)


def pack_kernel(vol, blocks, first, last, flat):
    flat[...] = vol[...].reshape(1024, 128).astype(F32)
    for z in range(2):
        for row in range(32):
            tile = flat[pl.ds(z * 32 + row, 16, stride=64), :].astype(BF)
            for chip in range(4):
                at = row - 15 * (chip % 2)
                if 0 <= at < 17:
                    blocks[chip, z * 17 + at] = tile
            if row == 0:
                first[pl.ds(z * 16, 16)] = tile
            if row == 31:
                last[pl.ds(z * 16, 16)] = tile


def beside_kernel(first, last, left, right, up, down, beside):
    lane = lanes_of((32, 128))
    both = jnp.where(
        lane < 32,
        pltpu.roll(left[...].astype(F32), 96, 1),
        jnp.where(lane < 64, pltpu.roll(right[...].astype(F32), 32, 1), 0.0),
    )
    beside[...] = both
    nothing = jnp.zeros((15, 128), F32)
    up[pl.ds(0, 32)] = last[...]
    up[pl.ds(32, 16)] = jnp.concatenate([both[31:32], nothing], axis=0).astype(BF)
    down[pl.ds(0, 32)] = first[...]
    down[pl.ds(32, 16)] = jnp.concatenate([both[0:1], nothing], axis=0).astype(BF)


def halo_kernel(above, below, beside, out, buf):
    buf[...] = jnp.zeros((40, 128), F32)
    buf[pl.ds(0, 1), :] = above[pl.ds(32, 16)].astype(F32)[0:1]
    buf[pl.ds(1, 32), :] = beside[...]
    buf[pl.ds(33, 1), :] = below[pl.ds(32, 16)].astype(F32)[0:1]
    lane = lanes_of((16, 128))
    sides = [
        jnp.where(
            lane < 64, buf[pl.ds(16 * half, 16), :], pltpu.roll(buf[pl.ds(16 * half + 8, 16), :], 64, 1)
        ).astype(BF)
        for half in range(2)
    ]
    for d in range(8):
        half = d // 2 % 2
        out[d, pl.ds(0, 32)] = below[pl.ds(0, 32)] if half else above[pl.ds(0, 32)]
        out[d, pl.ds(32, 16)] = sides[half]


def taps_kernel(own, other, taps, taps2):
    odd = lax.rem(lax.axis_index("ch"), 2) == 1
    even_block = lax.rem(lanes_of((16, 128)) // 16, 2) == 0
    for filters, to in ((own, taps), (other, taps2)):
        for a in range(3):
            for b in range(3):
                for e in range(3):
                    tile = filters[pl.ds((a * 9 + b * 3 + e) * 16, 16)].astype(F32)
                    swapped = jnp.where(even_block, pltpu.roll(tile, 112, 1), pltpu.roll(tile, 16, 1))
                    tile = jnp.where(odd, swapped, tile).astype(BF)
                    for zo in range(2):
                        zi = a - 1 + zo
                        if 0 <= zi < 2:
                            to[pl.ds(((b * 3 + e) * 2 + zo) * 16, 16), pl.ds(zi * 128, 128)] = tile


def half_of():
    return lax.rem(lax.axis_index("ch") // 2, 2)


def aligned(total, lane):
    before = jnp.where(lane == 0, 0.0, pltpu.roll(total[0:32], 1, 1))
    after = jnp.where(lane == 127, 0.0, pltpu.roll(total[64:96], 127, 1))
    return total[32:64] + (before + after)


def inner_kernel(mine, theirs, taps, taps2, pre, pre2, sums):
    half = half_of()
    lane = lanes_of((32, 128))

    def row_of(row):
        return jnp.concatenate(
            [held[chip, z * 17 + row + half] for z in range(2) for chip in range(4) for held in (mine, theirs)],
            axis=0,
        )

    for p in range(8):
        pair = jnp.concatenate([row_of(2 * p), row_of(2 * p + 1)], axis=1)
        for t, (weights, to) in enumerate(((taps, pre), (taps2, pre2))):
            got = jnp.dot(weights[...], pair, preferred_element_type=F32)
            for h in range(2):
                for b in range(3):
                    row = 2 * p + h + 1 - b
                    if not 0 <= row < 16:
                        continue
                    part = got[b * 96 : (b + 1) * 96, h * 128 : (h + 1) * 128]
                    if not (b == 0 or (b == 1 and row == 0)):
                        part = part + sums[t, row]
                    if b == 2 or (b == 1 and row == 15):
                        to[row] = aligned(part, lane)
                    else:
                        sums[t, row] = part


def outer_kernel(pre, taps, mine, theirs, halo, filters, out, flat):
    me = lax.axis_index("ch")
    half, core = half_of(), lax.rem(me, 2)
    parts = filters[pl.ds(432, 16)].astype(F32)
    offset = (parts[:, 0:1] + parts[:, 1:2]) + parts[:, 2:3]
    offset = jnp.concatenate([offset, offset], axis=0)
    sources = [2 * chip + (core ^ t) for chip in range(4) for t in range(2)]
    lane24 = lanes_of((24, 128))
    total = [[jnp.zeros((24, 128), F32) for _ in range(2)] for _ in range(2)]
    for j, source in enumerate(sources):
        both = halo[source, pl.ds(32, 16)].astype(F32)
        both = jnp.concatenate([both, pltpu.roll(both[8:16], 64, 1)], axis=0)
        for side in range(2):
            for z in range(2):
                shift = (j * 16 - side * 32 - z * 16) % 128
                piece = pltpu.roll(both, shift, 1) if shift else both
                total[side][z] = jnp.where(lane24 // 16 == j, piece, total[side][z])
    beside = jnp.concatenate(
        [jnp.concatenate(total[0], axis=1), jnp.concatenate(total[1], axis=1), jnp.zeros((80, 256), F32)], axis=0
    ).astype(BF)
    edge = lax.dot_general(taps[...], beside, (((1,), (1,)), ((), ())), preferred_element_type=F32)
    before, after = (
        edge[e * 32 : e * 32 + 32]
        + pltpu.roll(edge[96 + e * 32 : 128 + e * 32], 127, 1)
        + pltpu.roll(edge[192 + e * 32 : 224 + e * 32], 126, 1)
        for e in (0, 2)
    )
    lane = lanes_of((32, 128))
    far = jnp.concatenate(
        [halo[source, pl.ds(z * 16, 16)] for z in range(2) for source in sources], axis=0
    ).astype(F32)
    near = jnp.concatenate(
        [
            held[chip, z * 17 + 16 * (1 - half)]
            for z in range(2)
            for chip in range(4)
            for held in (mine, theirs)
        ],
        axis=0,
    ).astype(F32)
    first_half = half == 0
    above = jnp.where(first_half, far, near).astype(BF)
    below = jnp.where(first_half, near, far).astype(BF)
    above = aligned(jnp.dot(taps[pl.ds(0, 96)], above, preferred_element_type=F32), lane)
    below = aligned(jnp.dot(taps[pl.ds(192, 96)], below, preferred_element_type=F32), lane)
    for row in range(16):
        total = pre[row] + offset
        if row == 0:
            total = total + above
        if row == 15:
            total = total + below
        total = total + jnp.where(lane == 0, before[:, row : row + 1], 0.0)
        total = total + jnp.where(lane == 127, after[:, 24 + row : 25 + row], 0.0)
        total = jnp.where(total >= 0, total, 0.3 * total)
        for z in range(2):
            flat[pl.ds(z * 16 + row, 16, stride=32), :] = total[z * 16 : z * 16 + 16]
    out[...] = flat[...].reshape(16, 2, 16, 128).astype(BF)


def place(ready, out, start, sem):
    copy = pltpu.make_async_copy(ready, out.at[:, :, pl.ds(pl.multiple_of(start, 16), 16)], sem)
    copy.start()
    copy.wait()


def kept_kernel(pre, taps, mine, theirs, halo, filters, out, flat, ready, sem):
    outer_kernel(pre, taps, mine, theirs, halo, filters, ready, flat)
    place(ready, out, 16 * half_of(), sem)


def unpack_kernel(got, held, out, sem):
    place(got, out, 16 * (1 - half_of()), sem)


def shifts(array, axis, up=True):
    size = lax.axis_size(axis)
    pairs = [(i, i + 1) for i in range(size - 1)]
    return lax.ppermute(array, axis, pairs if up else [(j, i) for i, j in pairs])


def swapped(array, t):
    return lax.ppermute(array, "ch", [(d, d ^ t) for d in range(8)])


def thirds(bias):
    high = bias.astype(BF)
    rest = bias - high.astype(F32)
    middle = rest.astype(BF)
    low = (rest - middle.astype(F32)).astype(BF)
    return jnp.pad(jnp.stack([high, middle, low], axis=1), ((0, 0), (0, 125)))


def stages(volume, weights, bias):
    cols = call(columns_kernel, shaped(32, 128), [], volume, moved=1 << 19)
    blocks, first, last = call(
        pack_kernel,
        [shaped(4, 34, 16, 128), shaped(32, 128), shaped(32, 128)],
        [pltpu.VMEM((1024, 128), F32)],
        volume,
        moved=1 << 20,
    )
    mine = lax.all_to_all(blocks, "ch", split_axis=0, concat_axis=0, tiled=True, axis_index_groups=CORES)
    left = shifts(cols, "sy", True)
    right = shifts(cols, "sy", False)
    own = jnp.concatenate([weights.transpose(2, 3, 4, 0, 1).reshape(432, 128), thirds(bias)], axis=0)
    other = swapped(own, 2)
    up, down, beside = call(
        beside_kernel,
        [shaped(48, 128), shaped(48, 128), shaped(32, 128, dtype=F32)],
        [],
        first,
        last,
        left,
        right,
        moved=1 << 16,
    )
    above = shifts(up, "sx", True)
    below = shifts(down, "sx", False)
    theirs = swapped(mine, 1)
    taps, taps2 = call(taps_kernel, [shaped(288, 256)] * 2, [], own, other, moved=1 << 19)
    halo = call(halo_kernel, shaped(8, 48, 128), [pltpu.VMEM((40, 128), F32)], above, below, beside, moved=1 << 17)
    halo = lax.all_to_all(halo, "ch", split_axis=0, concat_axis=0, tiled=True)
    pre, pre2 = call(
        inner_kernel,
        [shaped(16, 32, 128, dtype=F32)] * 2,
        [pltpu.VMEM((2, 16, 96, 128), F32)],
        mine,
        theirs,
        taps,
        taps2,
        flops=2 * 576 * 256 * 2048,
        moved=3 << 20,
    )
    cost = dict(flops=2 * 288 * 256 * 256, moved=1 << 20)
    flat = pltpu.VMEM((512, 128), F32)
    ready, sem = pltpu.VMEM((16, 2, 16, 128), BF), pltpu.SemaphoreType.DMA
    space = pl.BlockSpec(memory_space=pl.ANY)
    sent = call(outer_kernel, shaped(16, 2, 16, 128), [flat], pre2, taps2, mine, theirs, halo, other, **cost)
    got = swapped(sent, 2)
    result = call(
        kept_kernel,
        shaped(16, 2, 32, 128),
        [flat, ready, sem],
        pre,
        taps,
        mine,
        theirs,
        halo,
        own,
        place=space,
        **cost,
    )
    return call(unpack_kernel, shaped(16, 2, 32, 128), [sem], got, result, moved=1 << 18, place=space, shared={1: 0})


def solution(mesh):
    in_specs = (P("ch", None, "sx", "sy"), P("ch", None, None, None, None), P("ch"))
    out_specs = P("ch", None, "sx", "sy")
    return jax.shard_map(stages, mesh=mesh, in_specs=in_specs, out_specs=out_specs, check_vma=False)
```

```python
import jax
import jax.numpy as jnp
from jax import lax
from jax.experimental import pallas as pl
from jax.experimental.pallas import tpu as pltpu
from jax.sharding import PartitionSpec as P


BF = jnp.bfloat16
F32 = jnp.float32
GRANT = 16 << 20


def call(kernel, out_shapes, scratch, *args, flops=0, moved=0, place=None, shared=None):
    vmem = pl.BlockSpec(memory_space=pltpu.VMEM)
    many = isinstance(out_shapes, (list, tuple))
    in_specs = [vmem] * len(args)
    for i in shared or {}:
        in_specs[i] = pl.BlockSpec(memory_space=pl.ANY)
    return pl.pallas_call(
        kernel,
        out_shape=out_shapes,
        in_specs=in_specs,
        out_specs=[vmem] * len(out_shapes) if many else place or vmem,
        scratch_shapes=scratch,
        input_output_aliases=shared or {},
        cost_estimate=pl.CostEstimate(flops=flops, bytes_accessed=moved, transcendentals=0),
        compiler_params=pltpu.CompilerParams(vmem_limit_bytes=GRANT),
    )(*args)


def shaped(*shape, dtype=BF):
    return jax.ShapeDtypeStruct(shape, dtype)


def lanes_of(shape):
    return lax.broadcasted_iota(jnp.int32, shape, len(shape) - 1)


def columns_kernel(vol, cols):
    lane = lanes_of((32, 128))
    both = jnp.zeros((32, 128), F32)
    for z in range(2):
        for c in range(16):
            tile = vol[c, z].astype(F32)
            j = z * 16 + c
            both = jnp.where(lane == j, pltpu.roll(tile, j, 1) if j else tile, both)
            both = jnp.where(lane == 32 + j, pltpu.roll(tile, 33 + j, 1), both)
    cols[...] = both.astype(BF)


def pack_kernel(vol, same, other, first, last, flat):
    half = half_of()
    flat[...] = vol[...].reshape(1024, 128).astype(F32)
    for to, start in ((same, 15 * half), (other, 15 * (1 - half))):
        for z in range(2):
            for i in range(17):
                to[z * 17 + i] = flat[pl.ds(start + z * 32 + i, 16, stride=64), :].astype(BF)
    for z in range(2):
        first[pl.ds(z * 16, 16)] = flat[pl.ds(z * 32, 16, stride=64), :].astype(BF)
        last[pl.ds(z * 16, 16)] = flat[pl.ds(z * 32 + 31, 16, stride=64), :].astype(BF)


def join_kernel(p0, p1, p2, p3, joined):
    for m, piece in enumerate((p0, p1, p2, p3)):
        joined[m] = piece[...]


def beside_kernel(first, last, left, right, up, down, beside):
    lane = lanes_of((32, 128))
    both = jnp.where(
        lane < 32,
        pltpu.roll(left[...].astype(F32), 96, 1),
        jnp.where(lane < 64, pltpu.roll(right[...].astype(F32), 32, 1), 0.0),
    )
    beside[...] = both
    nothing = jnp.zeros((15, 128), F32)
    up[pl.ds(0, 32)] = last[...]
    up[pl.ds(32, 16)] = jnp.concatenate([both[31:32], nothing], axis=0).astype(BF)
    down[pl.ds(0, 32)] = first[...]
    down[pl.ds(32, 16)] = jnp.concatenate([both[0:1], nothing], axis=0).astype(BF)


def halo_kernel(above, below, beside, out, buf):
    buf[...] = jnp.zeros((40, 128), F32)
    buf[pl.ds(0, 1), :] = above[pl.ds(32, 16)].astype(F32)[0:1]
    buf[pl.ds(1, 32), :] = beside[...]
    buf[pl.ds(33, 1), :] = below[pl.ds(32, 16)].astype(F32)[0:1]
    lane = lanes_of((16, 128))
    sides = [
        jnp.where(
            lane < 64, buf[pl.ds(16 * half, 16), :], pltpu.roll(buf[pl.ds(16 * half + 8, 16), :], 64, 1)
        ).astype(BF)
        for half in range(2)
    ]
    for d in range(8):
        half = d // 2 % 2
        out[d, pl.ds(0, 32)] = below[pl.ds(0, 32)] if half else above[pl.ds(0, 32)]
        out[d, pl.ds(32, 16)] = sides[half]


def taps_kernel(own, other, taps, taps2):
    me = lax.axis_index("ch")
    lane = lanes_of((16, 128))
    for filters, to in ((own, taps), (other, taps2)):
        for a in range(3):
            for b in range(3):
                for e in range(3):
                    tile = filters[pl.ds((a * 9 + b * 3 + e) * 16, 16)].astype(F32)
                    for bit in range(3):
                        width = 16 << bit
                        swapped = jnp.where(
                            lax.rem(lane // width, 2) == 0,
                            pltpu.roll(tile, 128 - width, 1),
                            pltpu.roll(tile, width, 1),
                        )
                        tile = jnp.where(lax.rem(me // (1 << bit), 2) == 1, swapped, tile)
                    tile = tile.astype(BF)
                    for zo in range(2):
                        zi = a - 1 + zo
                        if 0 <= zi < 2:
                            to[pl.ds(((b * 3 + e) * 2 + zo) * 16, 16), pl.ds(zi * 128, 128)] = tile


def half_of():
    return lax.rem(lax.axis_index("ch") // 2, 2)


def aligned(total, lane):
    before = jnp.where(lane == 0, 0.0, pltpu.roll(total[0:32], 1, 1))
    after = jnp.where(lane == 127, 0.0, pltpu.roll(total[64:96], 127, 1))
    return total[32:64] + (before + after)


def inner_kernel(mine, theirs, taps, taps2, pre, pre2, sums):
    half = half_of()
    lane = lanes_of((32, 128))

    def row_of(row):
        return jnp.concatenate(
            [held[chip, z * 17 + row + half] for z in range(2) for chip in range(4) for held in (mine, theirs)],
            axis=0,
        )

    for p in range(8):
        pair = jnp.concatenate([row_of(2 * p), row_of(2 * p + 1)], axis=1)
        for t, (weights, to) in enumerate(((taps, pre), (taps2, pre2))):
            got = jnp.dot(weights[...], pair, preferred_element_type=F32)
            for h in range(2):
                for b in range(3):
                    row = 2 * p + h + 1 - b
                    if not 0 <= row < 16:
                        continue
                    part = got[b * 96 : (b + 1) * 96, h * 128 : (h + 1) * 128]
                    if not (b == 0 or (b == 1 and row == 0)):
                        part = part + sums[t, row]
                    if b == 2 or (b == 1 and row == 15):
                        to[row] = aligned(part, lane)
                    else:
                        sums[t, row] = part


def outer_kernel(pre, taps, mine, theirs, halo, filters, out, flat):
    me = lax.axis_index("ch")
    half = half_of()
    parts = filters[pl.ds(432, 16)].astype(F32)
    offset = (parts[:, 0:1] + parts[:, 1:2]) + parts[:, 2:3]
    offset = jnp.concatenate([offset, offset], axis=0)
    sources = [me ^ j for j in range(8)]
    lane24 = lanes_of((24, 128))
    total = [[jnp.zeros((24, 128), F32) for _ in range(2)] for _ in range(2)]
    for j, source in enumerate(sources):
        both = halo[source, pl.ds(32, 16)].astype(F32)
        both = jnp.concatenate([both, pltpu.roll(both[8:16], 64, 1)], axis=0)
        for side in range(2):
            for z in range(2):
                shift = (j * 16 - side * 32 - z * 16) % 128
                piece = pltpu.roll(both, shift, 1) if shift else both
                total[side][z] = jnp.where(lane24 // 16 == j, piece, total[side][z])
    beside = jnp.concatenate(
        [jnp.concatenate(total[0], axis=1), jnp.concatenate(total[1], axis=1), jnp.zeros((80, 256), F32)], axis=0
    ).astype(BF)
    edge = lax.dot_general(taps[...], beside, (((1,), (1,)), ((), ())), preferred_element_type=F32)
    before, after = (
        edge[e * 32 : e * 32 + 32]
        + pltpu.roll(edge[96 + e * 32 : 128 + e * 32], 127, 1)
        + pltpu.roll(edge[192 + e * 32 : 224 + e * 32], 126, 1)
        for e in (0, 2)
    )
    lane = lanes_of((32, 128))
    far = jnp.concatenate(
        [halo[source, pl.ds(z * 16, 16)] for z in range(2) for source in sources], axis=0
    ).astype(F32)
    near = jnp.concatenate(
        [
            held[chip, z * 17 + 16 * (1 - half)]
            for z in range(2)
            for chip in range(4)
            for held in (mine, theirs)
        ],
        axis=0,
    ).astype(F32)
    first_half = half == 0
    above = jnp.where(first_half, far, near).astype(BF)
    below = jnp.where(first_half, near, far).astype(BF)
    above = aligned(jnp.dot(taps[pl.ds(0, 96)], above, preferred_element_type=F32), lane)
    below = aligned(jnp.dot(taps[pl.ds(192, 96)], below, preferred_element_type=F32), lane)
    for row in range(16):
        total = pre[row] + offset
        if row == 0:
            total = total + above
        if row == 15:
            total = total + below
        total = total + jnp.where(lane == 0, before[:, row : row + 1], 0.0)
        total = total + jnp.where(lane == 127, after[:, 24 + row : 25 + row], 0.0)
        total = jnp.where(total >= 0, total, 0.3 * total)
        for z in range(2):
            flat[pl.ds(z * 16 + row, 16, stride=32), :] = total[z * 16 : z * 16 + 16]
    out[...] = flat[...].reshape(16, 2, 16, 128).astype(BF)


def place(ready, out, start, sem):
    copy = pltpu.make_async_copy(ready, out.at[:, :, pl.ds(pl.multiple_of(start, 16), 16)], sem)
    copy.start()
    copy.wait()


def kept_kernel(pre, taps, mine, theirs, halo, filters, out, flat, ready, sem):
    outer_kernel(pre, taps, mine, theirs, halo, filters, ready, flat)
    place(ready, out, 16 * half_of(), sem)


def unpack_kernel(got, held, out, sem):
    place(got, out, 16 * (1 - half_of()), sem)


def shifts(array, axis, up=True):
    size = lax.axis_size(axis)
    pairs = [(i, i + 1) for i in range(size - 1)]
    return lax.ppermute(array, axis, pairs if up else [(j, i) for i, j in pairs])


def swapped(array, t):
    return lax.ppermute(array, "ch", [(d, d ^ t) for d in range(8)])


def thirds(bias):
    high = bias.astype(BF)
    rest = bias - high.astype(F32)
    middle = rest.astype(BF)
    low = (rest - middle.astype(F32)).astype(BF)
    return jnp.pad(jnp.stack([high, middle, low], axis=1), ((0, 0), (0, 125)))


def stages(volume, weights, bias):
    cols = call(columns_kernel, shaped(32, 128), [], volume, moved=1 << 19)
    same, rest, first, last = call(
        pack_kernel,
        [shaped(34, 16, 128), shaped(34, 16, 128), shaped(32, 128), shaped(32, 128)],
        [pltpu.VMEM((1024, 128), F32)],
        volume,
        moved=1 << 20,
    )
    piece3 = swapped(rest, 6)
    piece2 = swapped(same, 4)
    piece1 = swapped(rest, 2)
    mine = call(join_kernel, shaped(4, 34, 16, 128), [], same, piece1, piece2, piece3, moved=1 << 20)
    left = shifts(cols, "sy", True)
    right = shifts(cols, "sy", False)
    own = jnp.concatenate([weights.transpose(2, 3, 4, 0, 1).reshape(432, 128), thirds(bias)], axis=0)
    other = swapped(own, 2)
    up, down, beside = call(
        beside_kernel,
        [shaped(48, 128), shaped(48, 128), shaped(32, 128, dtype=F32)],
        [],
        first,
        last,
        left,
        right,
        moved=1 << 16,
    )
    above = shifts(up, "sx", True)
    below = shifts(down, "sx", False)
    theirs = swapped(mine, 1)
    taps, taps2 = call(taps_kernel, [shaped(288, 256)] * 2, [], own, other, moved=1 << 19)
    halo = call(halo_kernel, shaped(8, 48, 128), [pltpu.VMEM((40, 128), F32)], above, below, beside, moved=1 << 17)
    halo = lax.all_to_all(halo, "ch", split_axis=0, concat_axis=0, tiled=True)
    pre, pre2 = call(
        inner_kernel,
        [shaped(16, 32, 128, dtype=F32)] * 2,
        [pltpu.VMEM((2, 16, 96, 128), F32)],
        mine,
        theirs,
        taps,
        taps2,
        flops=2 * 576 * 256 * 2048,
        moved=3 << 20,
    )
    cost = dict(flops=2 * 288 * 256 * 256, moved=1 << 20)
    flat = pltpu.VMEM((512, 128), F32)
    ready, sem = pltpu.VMEM((16, 2, 16, 128), BF), pltpu.SemaphoreType.DMA
    space = pl.BlockSpec(memory_space=pl.ANY)
    sent = call(outer_kernel, shaped(16, 2, 16, 128), [flat], pre2, taps2, mine, theirs, halo, other, **cost)
    got = swapped(sent, 2)
    result = call(
        kept_kernel,
        shaped(16, 2, 32, 128),
        [flat, ready, sem],
        pre,
        taps,
        mine,
        theirs,
        halo,
        own,
        place=space,
        **cost,
    )
    return call(unpack_kernel, shaped(16, 2, 32, 128), [sem], got, result, moved=1 << 18, place=space, shared={1: 0})


def solution(mesh):
    in_specs = (P("ch", None, "sx", "sy"), P("ch", None, None, None, None), P("ch"))
    out_specs = P("ch", None, "sx", "sy")
    return jax.shard_map(stages, mesh=mesh, in_specs=in_specs, out_specs=out_specs, check_vma=False)
```

```python
import jax
import jax.numpy as jnp
from jax import lax
from jax.experimental import pallas as pl
from jax.experimental.pallas import tpu as pltpu
from jax.sharding import PartitionSpec as P


BF = jnp.bfloat16
F32 = jnp.float32
CORES = [[0, 2, 4, 6], [1, 3, 5, 7]]
GRANT = 16 << 20


def call(kernel, out_shapes, scratch, *args, flops=0, moved=0, far_in=(), far_out=(), shared=None):
    vmem, far = pl.BlockSpec(memory_space=pltpu.VMEM), pl.BlockSpec(memory_space=pl.ANY)
    many = isinstance(out_shapes, (list, tuple))
    outs = [far if i in far_out else vmem for i in range(len(out_shapes) if many else 1)]
    return pl.pallas_call(
        kernel,
        out_shape=out_shapes,
        in_specs=[far if i in far_in else vmem for i in range(len(args))],
        out_specs=outs if many else outs[0],
        scratch_shapes=scratch,
        input_output_aliases=shared or {},
        cost_estimate=pl.CostEstimate(flops=flops, bytes_accessed=moved, transcendentals=0),
        compiler_params=pltpu.CompilerParams(vmem_limit_bytes=GRANT),
    )(*args)


def shaped(*shape, dtype=BF):
    return jax.ShapeDtypeStruct(shape, dtype)


def lanes_of(shape):
    return lax.broadcasted_iota(jnp.int32, shape, len(shape) - 1)


def columns_kernel(vol, cols, held, sems):
    copies = [pltpu.make_async_copy(vol.at[c], held.at[c], sems.at[c]) for c in range(16)]
    for copy in copies:
        copy.start()
    lane = lanes_of((32, 128))
    both = jnp.zeros((32, 128), F32)
    for c in range(16):
        copies[c].wait()
        for z in range(2):
            tile = held[c, z].astype(F32)
            j = z * 16 + c
            both = jnp.where(lane == j, pltpu.roll(tile, j, 1) if j else tile, both)
            both = jnp.where(lane == 32 + j, pltpu.roll(tile, 33 + j, 1), both)
    cols[...] = both.astype(BF)


def pack_kernel(vol, blocks, first, last, flat, halves, sems):
    flat[...] = vol[...].reshape(1024, 128).astype(F32)
    copies = []
    for z in range(2):
        for half in range(2):
            for at in range(17):
                row = 15 * half + at
                tile = flat[pl.ds(z * 32 + row, 16, stride=64), :].astype(BF)
                halves[half, z * 17 + at] = tile
                if row == 0:
                    first[pl.ds(z * 16, 16)] = tile
                if row == 31:
                    last[pl.ds(z * 16, 16)] = tile
            part = pl.ds(z * 17, 17)
            for chip in (half, half + 2):
                copy = pltpu.make_async_copy(
                    halves.at[half, part], blocks.at[chip, part], sems.at[len(copies)]
                )
                copy.start()
                copies.append(copy)
    for copy in copies:
        copy.wait()


def beside_kernel(first, last, left, right, up, down, beside):
    lane = lanes_of((32, 128))
    both = jnp.where(
        lane < 32,
        pltpu.roll(left[...].astype(F32), 96, 1),
        jnp.where(lane < 64, pltpu.roll(right[...].astype(F32), 32, 1), 0.0),
    )
    beside[...] = both
    nothing = jnp.zeros((15, 128), F32)
    up[pl.ds(0, 32)] = last[...]
    up[pl.ds(32, 16)] = jnp.concatenate([both[31:32], nothing], axis=0).astype(BF)
    down[pl.ds(0, 32)] = first[...]
    down[pl.ds(32, 16)] = jnp.concatenate([both[0:1], nothing], axis=0).astype(BF)


def halo_kernel(above, below, beside, out, buf):
    buf[...] = jnp.zeros((40, 128), F32)
    buf[pl.ds(0, 1), :] = above[pl.ds(32, 16)].astype(F32)[0:1]
    buf[pl.ds(1, 32), :] = beside[...]
    buf[pl.ds(33, 1), :] = below[pl.ds(32, 16)].astype(F32)[0:1]
    lane = lanes_of((16, 128))
    sides = [
        jnp.where(
            lane < 64, buf[pl.ds(16 * half, 16), :], pltpu.roll(buf[pl.ds(16 * half + 8, 16), :], 64, 1)
        ).astype(BF)
        for half in range(2)
    ]
    for d in range(8):
        half = d // 2 % 2
        out[d, pl.ds(0, 32)] = below[pl.ds(0, 32)] if half else above[pl.ds(0, 32)]
        out[d, pl.ds(32, 16)] = sides[half]


def taps_kernel(own, other, taps, taps2):
    odd = lax.rem(lax.axis_index("ch"), 2) == 1
    even_block = lax.rem(lanes_of((16, 128)) // 16, 2) == 0
    for filters, to in ((own, taps), (other, taps2)):
        for a in range(3):
            for b in range(3):
                for e in range(3):
                    tile = filters[pl.ds((a * 9 + b * 3 + e) * 16, 16)].astype(F32)
                    swapped = jnp.where(even_block, pltpu.roll(tile, 112, 1), pltpu.roll(tile, 16, 1))
                    tile = jnp.where(odd, swapped, tile).astype(BF)
                    for zo in range(2):
                        zi = a - 1 + zo
                        if 0 <= zi < 2:
                            to[pl.ds(((b * 3 + e) * 2 + zo) * 16, 16), pl.ds(zi * 128, 128)] = tile


def half_of():
    return lax.rem(lax.axis_index("ch") // 2, 2)


def aligned(total, lane):
    before = jnp.where(lane == 0, 0.0, pltpu.roll(total[0:32], 1, 1))
    after = jnp.where(lane == 127, 0.0, pltpu.roll(total[64:96], 127, 1))
    return total[32:64] + (before + after)


def inner_kernel(mine, theirs, taps, taps2, pre, pre2, sums):
    half = half_of()
    lane = lanes_of((32, 128))

    def row_of(row):
        return jnp.concatenate(
            [held[chip, z * 17 + row + half] for z in range(2) for chip in range(4) for held in (mine, theirs)],
            axis=0,
        )

    for p in range(8):
        pair = jnp.concatenate([row_of(2 * p), row_of(2 * p + 1)], axis=1)
        for t, (weights, to) in enumerate(((taps, pre), (taps2, pre2))):
            got = jnp.dot(weights[...], pair, preferred_element_type=F32)
            for h in range(2):
                for b in range(3):
                    row = 2 * p + h + 1 - b
                    if not 0 <= row < 16:
                        continue
                    part = got[b * 96 : (b + 1) * 96, h * 128 : (h + 1) * 128]
                    if not (b == 0 or (b == 1 and row == 0)):
                        part = part + sums[t, row]
                    if b == 2 or (b == 1 and row == 15):
                        to[row] = aligned(part, lane)
                    else:
                        sums[t, row] = part


def outer_kernel(pre, taps, mine, theirs, halo, filters, out, flat):
    me = lax.axis_index("ch")
    half, core = half_of(), lax.rem(me, 2)
    parts = filters[pl.ds(432, 16)].astype(F32)
    offset = (parts[:, 0:1] + parts[:, 1:2]) + parts[:, 2:3]
    offset = jnp.concatenate([offset, offset], axis=0)
    sources = [2 * chip + (core ^ t) for chip in range(4) for t in range(2)]
    lane24 = lanes_of((24, 128))
    total = [[jnp.zeros((24, 128), F32) for _ in range(2)] for _ in range(2)]
    for j, source in enumerate(sources):
        both = halo[source, pl.ds(32, 16)].astype(F32)
        both = jnp.concatenate([both, pltpu.roll(both[8:16], 64, 1)], axis=0)
        for side in range(2):
            for z in range(2):
                shift = (j * 16 - side * 32 - z * 16) % 128
                piece = pltpu.roll(both, shift, 1) if shift else both
                total[side][z] = jnp.where(lane24 // 16 == j, piece, total[side][z])
    beside = jnp.concatenate(
        [jnp.concatenate(total[0], axis=1), jnp.concatenate(total[1], axis=1), jnp.zeros((80, 256), F32)], axis=0
    ).astype(BF)
    edge = lax.dot_general(taps[...], beside, (((1,), (1,)), ((), ())), preferred_element_type=F32)
    before, after = (
        edge[e * 32 : e * 32 + 32]
        + pltpu.roll(edge[96 + e * 32 : 128 + e * 32], 127, 1)
        + pltpu.roll(edge[192 + e * 32 : 224 + e * 32], 126, 1)
        for e in (0, 2)
    )
    lane = lanes_of((32, 128))
    far = jnp.concatenate(
        [halo[source, pl.ds(z * 16, 16)] for z in range(2) for source in sources], axis=0
    ).astype(F32)
    near = jnp.concatenate(
        [
            held[chip, z * 17 + 16 * (1 - half)]
            for z in range(2)
            for chip in range(4)
            for held in (mine, theirs)
        ],
        axis=0,
    ).astype(F32)
    first_half = half == 0
    above = jnp.where(first_half, far, near).astype(BF)
    below = jnp.where(first_half, near, far).astype(BF)
    above = aligned(jnp.dot(taps[pl.ds(0, 96)], above, preferred_element_type=F32), lane)
    below = aligned(jnp.dot(taps[pl.ds(192, 96)], below, preferred_element_type=F32), lane)
    for row in range(16):
        total = pre[row] + offset
        if row == 0:
            total = total + above
        if row == 15:
            total = total + below
        total = total + jnp.where(lane == 0, before[:, row : row + 1], 0.0)
        total = total + jnp.where(lane == 127, after[:, 24 + row : 25 + row], 0.0)
        total = jnp.where(total >= 0, total, 0.3 * total)
        for z in range(2):
            flat[pl.ds(z * 16 + row, 16, stride=32), :] = total[z * 16 : z * 16 + 16]
    out[...] = flat[...].reshape(16, 2, 16, 128).astype(BF)


def place(ready, out, start, sems):
    rows = pl.ds(pl.multiple_of(start, 16), 16)
    copies = [
        pltpu.make_async_copy(
            ready.at[pl.ds(4 * i, 4)], out.at[pl.ds(4 * i, 4), :, rows], sems.at[i]
        )
        for i in range(4)
    ]
    for copy in copies:
        copy.start()
    for copy in copies:
        copy.wait()


def kept_kernel(pre, taps, mine, theirs, halo, filters, out, flat, ready, sem):
    outer_kernel(pre, taps, mine, theirs, halo, filters, ready, flat)
    place(ready, out, 16 * half_of(), sem)


def unpack_kernel(got, held, out, sem):
    place(got, out, 16 * (1 - half_of()), sem)


def shifts(array, axis, up=True):
    size = lax.axis_size(axis)
    pairs = [(i, i + 1) for i in range(size - 1)]
    return lax.ppermute(array, axis, pairs if up else [(j, i) for i, j in pairs])


def swapped(array, t):
    return lax.ppermute(array, "ch", [(d, d ^ t) for d in range(8)])


def thirds(bias):
    high = bias.astype(BF)
    rest = bias - high.astype(F32)
    middle = rest.astype(BF)
    low = (rest - middle.astype(F32)).astype(BF)
    return jnp.pad(jnp.stack([high, middle, low], axis=1), ((0, 0), (0, 125)))


def stages(volume, weights, bias):
    cols = call(
        columns_kernel,
        shaped(32, 128),
        [pltpu.VMEM((16, 2, 32, 128), BF), pltpu.SemaphoreType.DMA((16,))],
        volume,
        moved=1 << 18,
        far_in=(0,),
    )
    blocks, first, last = call(
        pack_kernel,
        [shaped(4, 34, 16, 128), shaped(32, 128), shaped(32, 128)],
        [pltpu.VMEM((1024, 128), F32), pltpu.VMEM((2, 34, 16, 128), BF), pltpu.SemaphoreType.DMA((8,))],
        volume,
        moved=1 << 20,
        far_out=(0,),
    )
    mine = lax.all_to_all(blocks, "ch", split_axis=0, concat_axis=0, tiled=True, axis_index_groups=CORES)
    left = shifts(cols, "sy", True)
    right = shifts(cols, "sy", False)
    own = jnp.concatenate([weights.transpose(2, 3, 4, 0, 1).reshape(432, 128), thirds(bias)], axis=0)
    other = swapped(own, 2)
    up, down, beside = call(
        beside_kernel,
        [shaped(48, 128), shaped(48, 128), shaped(32, 128, dtype=F32)],
        [],
        first,
        last,
        left,
        right,
        moved=1 << 16,
    )
    above = shifts(up, "sx", True)
    below = shifts(down, "sx", False)
    theirs = swapped(mine, 1)
    taps, taps2 = call(taps_kernel, [shaped(288, 256)] * 2, [], own, other, moved=1 << 19)
    halo = call(halo_kernel, shaped(8, 48, 128), [pltpu.VMEM((40, 128), F32)], above, below, beside, moved=1 << 17)
    halo = lax.all_to_all(halo, "ch", split_axis=0, concat_axis=0, tiled=True)
    pre, pre2 = call(
        inner_kernel,
        [shaped(16, 32, 128, dtype=F32)] * 2,
        [pltpu.VMEM((2, 16, 96, 128), F32)],
        mine,
        theirs,
        taps,
        taps2,
        flops=2 * 576 * 256 * 2048,
        moved=3 << 20,
    )
    cost = dict(flops=2 * 288 * 256 * 256, moved=1 << 20)
    flat = pltpu.VMEM((512, 128), F32)
    ready, sem = pltpu.VMEM((16, 2, 16, 128), BF), pltpu.SemaphoreType.DMA((4,))
    sent = call(outer_kernel, shaped(16, 2, 16, 128), [flat], pre2, taps2, mine, theirs, halo, other, **cost)
    got = swapped(sent, 2)
    result = call(
        kept_kernel,
        shaped(16, 2, 32, 128),
        [flat, ready, sem],
        pre,
        taps,
        mine,
        theirs,
        halo,
        own,
        far_out=(0,),
        **cost,
    )
    return call(
        unpack_kernel,
        shaped(16, 2, 32, 128),
        [sem],
        got,
        result,
        moved=1 << 18,
        far_in=(1,),
        far_out=(0,),
        shared={1: 0},
    )


def solution(mesh):
    in_specs = (P("ch", None, "sx", "sy"), P("ch", None, None, None, None), P("ch"))
    out_specs = P("ch", None, "sx", "sy")
    return jax.shard_map(stages, mesh=mesh, in_specs=in_specs, out_specs=out_specs, check_vma=False)
```

```python
import jax
import jax.numpy as jnp
from jax import lax
from jax.experimental import pallas as pl
from jax.experimental.pallas import tpu as pltpu
from jax.sharding import PartitionSpec as P


BF = jnp.bfloat16
F32 = jnp.float32
CORES = [[0, 2, 4, 6], [1, 3, 5, 7]]
GRANT = 16 << 20


def call(kernel, out_shapes, scratch, *args, flops=0, moved=0, place=None, shared=None):
    vmem = pl.BlockSpec(memory_space=pltpu.VMEM)
    many = isinstance(out_shapes, (list, tuple))
    in_specs = [vmem] * len(args)
    for i in shared or {}:
        in_specs[i] = pl.BlockSpec(memory_space=pl.ANY)
    return pl.pallas_call(
        kernel,
        out_shape=out_shapes,
        in_specs=in_specs,
        out_specs=[vmem] * len(out_shapes) if many else place or vmem,
        scratch_shapes=scratch,
        input_output_aliases=shared or {},
        cost_estimate=pl.CostEstimate(flops=flops, bytes_accessed=moved, transcendentals=0),
        compiler_params=pltpu.CompilerParams(vmem_limit_bytes=GRANT),
    )(*args)


def shaped(*shape, dtype=BF):
    return jax.ShapeDtypeStruct(shape, dtype)


def lanes_of(shape):
    return lax.broadcasted_iota(jnp.int32, shape, len(shape) - 1)


def columns_kernel(vol, cols):
    lane = lanes_of((32, 128))
    both = jnp.zeros((32, 128), F32)
    for z in range(2):
        for c in range(16):
            tile = vol[c, z].astype(F32)
            j = z * 16 + c
            both = jnp.where(lane == j, pltpu.roll(tile, j, 1) if j else tile, both)
            both = jnp.where(lane == 32 + j, pltpu.roll(tile, 33 + j, 1), both)
    cols[...] = both.astype(BF)


def pack_kernel(vol, blocks, first, last, flat):
    flat[...] = vol[...].reshape(1024, 128).astype(F32)
    for z in range(2):
        for row in range(32):
            tile = flat[pl.ds(z * 32 + row, 16, stride=64), :].astype(BF)
            for chip in range(4):
                at = row - 15 * (chip % 2)
                if 0 <= at < 17:
                    blocks[chip, z * 17 + at] = tile
            if row == 0:
                first[pl.ds(z * 16, 16)] = tile
            if row == 31:
                last[pl.ds(z * 16, 16)] = tile


def beside_kernel(first, last, left, right, up, down, beside):
    lane = lanes_of((32, 128))
    both = jnp.where(
        lane < 32,
        pltpu.roll(left[...].astype(F32), 96, 1),
        jnp.where(lane < 64, pltpu.roll(right[...].astype(F32), 32, 1), 0.0),
    )
    beside[...] = both
    nothing = jnp.zeros((15, 128), F32)
    up[pl.ds(0, 32)] = last[...]
    up[pl.ds(32, 16)] = jnp.concatenate([both[31:32], nothing], axis=0).astype(BF)
    down[pl.ds(0, 32)] = first[...]
    down[pl.ds(32, 16)] = jnp.concatenate([both[0:1], nothing], axis=0).astype(BF)


def halo_kernel(above, below, beside, out, buf):
    buf[...] = jnp.zeros((40, 128), F32)
    buf[pl.ds(0, 1), :] = above[pl.ds(32, 16)].astype(F32)[0:1]
    buf[pl.ds(1, 32), :] = beside[...]
    buf[pl.ds(33, 1), :] = below[pl.ds(32, 16)].astype(F32)[0:1]
    lane = lanes_of((16, 128))
    sides = [
        jnp.where(
            lane < 64, buf[pl.ds(16 * half, 16), :], pltpu.roll(buf[pl.ds(16 * half + 8, 16), :], 64, 1)
        ).astype(BF)
        for half in range(2)
    ]
    for d in range(8):
        half = d // 2 % 2
        out[d, pl.ds(0, 32)] = below[pl.ds(0, 32)] if half else above[pl.ds(0, 32)]
        out[d, pl.ds(32, 16)] = sides[half]


def taps_kernel(own, other, taps, taps2):
    odd = lax.rem(lax.axis_index("ch"), 2) == 1
    even_block = lax.rem(lanes_of((16, 128)) // 16, 2) == 0
    for filters, to in ((own, taps), (other, taps2)):
        for a in range(3):
            for b in range(3):
                for e in range(3):
                    tile = filters[pl.ds((a * 9 + b * 3 + e) * 16, 16)].astype(F32)
                    swapped = jnp.where(even_block, pltpu.roll(tile, 112, 1), pltpu.roll(tile, 16, 1))
                    tile = jnp.where(odd, swapped, tile).astype(BF)
                    for zo in range(2):
                        zi = a - 1 + zo
                        if 0 <= zi < 2:
                            to[pl.ds(((b * 3 + e) * 2 + zo) * 16, 16), pl.ds(zi * 128, 128)] = tile


def half_of():
    return lax.rem(lax.axis_index("ch") // 2, 2)


def aligned(total, lane):
    before = jnp.where(lane == 0, 0.0, pltpu.roll(total[0:32], 1, 1))
    after = jnp.where(lane == 127, 0.0, pltpu.roll(total[64:96], 127, 1))
    return total[32:64] + (before + after)


def offset_of(filters):
    parts = filters[pl.ds(432, 16)].astype(F32)
    offset = (parts[:, 0:1] + parts[:, 1:2]) + parts[:, 2:3]
    return jnp.concatenate([offset, offset], axis=0)


def activated(total):
    return jnp.where(total >= 0, total, 0.3 * total)


def inner_kernel(mine, theirs, taps, taps2, other, pre, pre2, early, sums):
    half = half_of()
    lane = lanes_of((32, 128))

    def row_of(row):
        return jnp.concatenate(
            [held[chip, z * 17 + row] for z in range(2) for chip in range(4) for held in (mine, theirs)],
            axis=0,
        )

    near = row_of(16 * (1 - half))
    for weights, to in ((taps, pre), (taps2, pre2)):
        ends = [
            aligned(jnp.dot(weights[pl.ds(b * 96, 96)], near, preferred_element_type=F32), lane) for b in (0, 2)
        ]
        to[0] = jnp.where(half == 1, ends[0], 0.0)
        to[15] = jnp.where(half == 0, ends[1], 0.0)
    offset = offset_of(other)
    for p in range(8):
        pair = jnp.concatenate([row_of(2 * p + half), row_of(2 * p + 1 + half)], axis=1)
        for t, (weights, to) in enumerate(((taps, pre), (taps2, pre2))):
            got = jnp.dot(weights[...], pair, preferred_element_type=F32)
            for h in range(2):
                for b in range(3):
                    row = 2 * p + h + 1 - b
                    if not 0 <= row < 16:
                        continue
                    part = got[b * 96 : (b + 1) * 96, h * 128 : (h + 1) * 128]
                    if not (b == 0 or (b == 1 and row == 0)):
                        part = part + sums[t, row]
                    if b == 2 or (b == 1 and row == 15):
                        total = aligned(part, lane)
                        if row in (0, 15):
                            total = total + to[row]
                        to[row] = total
                        if t == 1:
                            done = activated(total + offset).astype(BF)
                            for z in range(2):
                                early[z * 16 + row] = done[z * 16 : z * 16 + 16]
                    else:
                        sums[t, row] = part


def ends_of(taps, halo):
    me = lax.axis_index("ch")
    half = half_of()
    sources = [2 * chip + (lax.rem(me, 2) ^ t) for chip in range(4) for t in range(2)]
    lane24 = lanes_of((24, 128))
    total = [[jnp.zeros((24, 128), F32) for _ in range(2)] for _ in range(2)]
    for j, source in enumerate(sources):
        both = halo[source, pl.ds(32, 16)].astype(F32)
        both = jnp.concatenate([both, pltpu.roll(both[8:16], 64, 1)], axis=0)
        for side in range(2):
            for z in range(2):
                shift = (j * 16 - side * 32 - z * 16) % 128
                piece = pltpu.roll(both, shift, 1) if shift else both
                total[side][z] = jnp.where(lane24 // 16 == j, piece, total[side][z])
    beside = jnp.concatenate(
        [jnp.concatenate(total[0], axis=1), jnp.concatenate(total[1], axis=1), jnp.zeros((80, 256), F32)], axis=0
    ).astype(BF)
    edge = lax.dot_general(taps[...], beside, (((1,), (1,)), ((), ())), preferred_element_type=F32)
    before, after = (
        edge[e * 32 : e * 32 + 32]
        + pltpu.roll(edge[96 + e * 32 : 128 + e * 32], 127, 1)
        + pltpu.roll(edge[192 + e * 32 : 224 + e * 32], 126, 1)
        for e in (0, 2)
    )
    lane = lanes_of((32, 128))
    far = jnp.concatenate(
        [halo[source, pl.ds(z * 16, 16)] for z in range(2) for source in sources], axis=0
    )
    far = [aligned(jnp.dot(taps[pl.ds(b * 96, 96)], far, preferred_element_type=F32), lane) for b in (0, 2)]
    return jnp.where(half == 0, far[0], 0.0), jnp.where(half == 1, far[1], 0.0), before, after


def patch_kernel(pre, taps, halo, filters, patch):
    half = half_of()
    above, below, before, after = ends_of(taps, halo)
    offset = offset_of(filters)
    lane = lanes_of((32, 128))
    sides = jnp.zeros((32, 128), F32)
    end = jnp.zeros((32, 128), F32)
    for row in range(16):
        total = pre[row] + offset
        if row == 0:
            total = total + above
        if row == 15:
            total = total + below
        first = total[:, 0:1] + before[:, row : row + 1]
        last = total[:, 127:128] + after[:, 24 + row : 25 + row]
        sides = jnp.where(lane == row, first, sides)
        sides = jnp.where(lane == 64 + row, last, sides)
        if row in (0, 15):
            end = jnp.where(half == (row != 0), total, end)
    patch[pl.ds(0, 32)] = activated(end).astype(BF)
    patch[pl.ds(32, 32)] = activated(sides).astype(BF)


def outer_kernel(pre, taps, halo, filters, out, flat):
    above, below, before, after = ends_of(taps, halo)
    offset = offset_of(filters)
    lane = lanes_of((32, 128))
    for row in range(16):
        total = pre[row] + offset
        if row == 0:
            total = total + above
        if row == 15:
            total = total + below
        total = total + jnp.where(lane == 0, before[:, row : row + 1], 0.0)
        total = total + jnp.where(lane == 127, after[:, 24 + row : 25 + row], 0.0)
        total = activated(total)
        for z in range(2):
            flat[pl.ds(z * 16 + row, 16, stride=32), :] = total[z * 16 : z * 16 + 16]
    out[...] = flat[...].reshape(16, 2, 16, 128).astype(BF)


def place(ready, out, start, sem):
    copy = pltpu.make_async_copy(ready, out.at[:, :, pl.ds(pl.multiple_of(start, 16), 16)], sem)
    copy.start()
    copy.wait()


def kept_kernel(pre, taps, halo, filters, out, flat, ready, sem):
    outer_kernel(pre, taps, halo, filters, ready, flat)
    place(ready, out, 16 * half_of(), sem)


def unpack_kernel(got, patch, held, out, flat, ready, sem):
    half = half_of()
    lane = lanes_of((16, 128))
    for z in range(2):
        end = patch[pl.ds(z * 16, 16)].astype(F32)
        sides = patch[pl.ds(32 + z * 16, 16)].astype(F32)
        for row in range(16):
            tile = got[z * 16 + row].astype(F32)
            if row in (0, 15):
                tile = jnp.where(half == (row == 0), end, tile)
            tile = jnp.where(lane == 0, sides[:, row : row + 1], tile)
            tile = jnp.where(lane == 127, sides[:, 64 + row : 65 + row], tile)
            flat[pl.ds(z * 16 + row, 16, stride=32), :] = tile
    ready[...] = flat[...].reshape(16, 2, 16, 128).astype(BF)
    place(ready, out, 16 * (1 - half), sem)


def shifts(array, axis, up=True):
    size = lax.axis_size(axis)
    pairs = [(i, i + 1) for i in range(size - 1)]
    return lax.ppermute(array, axis, pairs if up else [(j, i) for i, j in pairs])


def swapped(array, t):
    return lax.ppermute(array, "ch", [(d, d ^ t) for d in range(8)])


def thirds(bias):
    high = bias.astype(BF)
    rest = bias - high.astype(F32)
    middle = rest.astype(BF)
    low = (rest - middle.astype(F32)).astype(BF)
    return jnp.pad(jnp.stack([high, middle, low], axis=1), ((0, 0), (0, 125)))


def stages(volume, weights, bias):
    cols = call(columns_kernel, shaped(32, 128), [], volume, moved=1 << 19)
    blocks, first, last = call(
        pack_kernel,
        [shaped(4, 34, 16, 128), shaped(32, 128), shaped(32, 128)],
        [pltpu.VMEM((1024, 128), F32)],
        volume,
        moved=1 << 20,
    )
    mine = lax.all_to_all(blocks, "ch", split_axis=0, concat_axis=0, tiled=True, axis_index_groups=CORES)
    left = shifts(cols, "sy", True)
    right = shifts(cols, "sy", False)
    own = jnp.concatenate([weights.transpose(2, 3, 4, 0, 1).reshape(432, 128), thirds(bias)], axis=0)
    other = swapped(own, 2)
    up, down, beside = call(
        beside_kernel,
        [shaped(48, 128), shaped(48, 128), shaped(32, 128, dtype=F32)],
        [],
        first,
        last,
        left,
        right,
        moved=1 << 16,
    )
    above = shifts(up, "sx", True)
    below = shifts(down, "sx", False)
    theirs = swapped(mine, 1)
    taps, taps2 = call(taps_kernel, [shaped(288, 256)] * 2, [], own, other, moved=1 << 19)
    halo = call(halo_kernel, shaped(8, 48, 128), [pltpu.VMEM((40, 128), F32)], above, below, beside, moved=1 << 17)
    halo = lax.all_to_all(halo, "ch", split_axis=0, concat_axis=0, tiled=True)
    pre, pre2, early = call(
        inner_kernel,
        [shaped(16, 32, 128, dtype=F32)] * 2 + [shaped(32, 16, 128)],
        [pltpu.VMEM((2, 16, 96, 128), F32)],
        mine,
        theirs,
        taps,
        taps2,
        other,
        flops=2 * 576 * 256 * 2048,
        moved=3 << 20,
    )
    cost = dict(flops=2 * 288 * 256 * 256, moved=1 << 20)
    flat = pltpu.VMEM((512, 128), F32)
    ready, sem = pltpu.VMEM((16, 2, 16, 128), BF), pltpu.SemaphoreType.DMA
    space = pl.BlockSpec(memory_space=pl.ANY)
    got = swapped(early, 2)
    patch = call(patch_kernel, shaped(64, 128), [], pre2, taps2, halo, other, **cost)
    patch = swapped(patch, 2)
    result = call(kept_kernel, shaped(16, 2, 32, 128), [flat, ready, sem], pre, taps, halo, own, place=space, **cost)
    return call(
        unpack_kernel,
        shaped(16, 2, 32, 128),
        [flat, ready, sem],
        got,
        patch,
        result,
        moved=1 << 18,
        place=space,
        shared={2: 0},
    )


def solution(mesh):
    in_specs = (P("ch", None, "sx", "sy"), P("ch", None, None, None, None), P("ch"))
    out_specs = P("ch", None, "sx", "sy")
    return jax.shard_map(stages, mesh=mesh, in_specs=in_specs, out_specs=out_specs, check_vma=False)
```

```python
import jax
import jax.numpy as jnp
from jax import lax
from jax.experimental import pallas as pl
from jax.experimental.pallas import tpu as pltpu
from jax.sharding import PartitionSpec as P


BF = jnp.bfloat16
F32 = jnp.float32
CORES = [[0, 2, 4, 6], [1, 3, 5, 7]]
GRANT = 16 << 20


def call(kernel, out_shapes, scratch, *args, flops=0, moved=0, place=None, shared=None):
    vmem = pl.BlockSpec(memory_space=pltpu.VMEM)
    many = isinstance(out_shapes, (list, tuple))
    in_specs = [vmem] * len(args)
    for i in shared or {}:
        in_specs[i] = pl.BlockSpec(memory_space=pl.ANY)
    return pl.pallas_call(
        kernel,
        out_shape=out_shapes,
        in_specs=in_specs,
        out_specs=[vmem] * len(out_shapes) if many else place or vmem,
        scratch_shapes=scratch,
        input_output_aliases=shared or {},
        cost_estimate=pl.CostEstimate(flops=flops, bytes_accessed=moved, transcendentals=0),
        compiler_params=pltpu.CompilerParams(vmem_limit_bytes=GRANT),
    )(*args)


def shaped(*shape, dtype=BF):
    return jax.ShapeDtypeStruct(shape, dtype)


def lanes_of(shape):
    return lax.broadcasted_iota(jnp.int32, shape, len(shape) - 1)


def columns_kernel(vol, cols):
    lane = lanes_of((32, 128))
    both = jnp.zeros((32, 128), F32)
    for z in range(2):
        for c in range(16):
            tile = vol[c, z].astype(F32)
            j = z * 16 + c
            both = jnp.where(lane == j, pltpu.roll(tile, j, 1) if j else tile, both)
            both = jnp.where(lane == 32 + j, pltpu.roll(tile, 33 + j, 1), both)
    cols[...] = both.astype(BF)


def pack_kernel(vol, blocks, first, last, flat):
    flat[...] = vol[...].reshape(1024, 128).astype(F32)
    for z in range(2):
        for row in range(32):
            tile = flat[pl.ds(z * 32 + row, 16, stride=64), :].astype(BF)
            for chip in range(4):
                at = row - 15 * (chip % 2)
                if 0 <= at < 17:
                    blocks[chip, z * 17 + at] = tile
            if row == 0:
                first[pl.ds(z * 16, 16)] = tile
            if row == 31:
                last[pl.ds(z * 16, 16)] = tile


def beside_kernel(first, last, left, right, up, down, beside):
    lane = lanes_of((32, 128))
    both = jnp.where(
        lane < 32,
        pltpu.roll(left[...].astype(F32), 96, 1),
        jnp.where(lane < 64, pltpu.roll(right[...].astype(F32), 32, 1), 0.0),
    )
    beside[...] = both
    nothing = jnp.zeros((15, 128), F32)
    up[pl.ds(0, 32)] = last[...]
    up[pl.ds(32, 16)] = jnp.concatenate([both[31:32], nothing], axis=0).astype(BF)
    down[pl.ds(0, 32)] = first[...]
    down[pl.ds(32, 16)] = jnp.concatenate([both[0:1], nothing], axis=0).astype(BF)


def halo_kernel(above, below, beside, out, buf):
    buf[...] = jnp.zeros((40, 128), F32)
    buf[pl.ds(0, 1), :] = above[pl.ds(32, 16)].astype(F32)[0:1]
    buf[pl.ds(1, 32), :] = beside[...]
    buf[pl.ds(33, 1), :] = below[pl.ds(32, 16)].astype(F32)[0:1]
    lane = lanes_of((16, 128))
    sides = [
        jnp.where(
            lane < 64, buf[pl.ds(16 * half, 16), :], pltpu.roll(buf[pl.ds(16 * half + 8, 16), :], 64, 1)
        ).astype(BF)
        for half in range(2)
    ]
    for d in range(8):
        half = d // 2 % 2
        out[d, pl.ds(0, 32)] = below[pl.ds(0, 32)] if half else above[pl.ds(0, 32)]
        out[d, pl.ds(32, 16)] = sides[half]


def taps_kernel(own, other, taps, taps2):
    odd = lax.rem(lax.axis_index("ch"), 2) == 1
    even_block = lax.rem(lanes_of((16, 128)) // 16, 2) == 0
    for filters, to in ((own, taps), (other, taps2)):
        for a in range(3):
            for b in range(3):
                for e in range(3):
                    tile = filters[pl.ds((a * 9 + b * 3 + e) * 16, 16)].astype(F32)
                    swapped = jnp.where(even_block, pltpu.roll(tile, 112, 1), pltpu.roll(tile, 16, 1))
                    tile = jnp.where(odd, swapped, tile).astype(BF)
                    for zo in range(2):
                        zi = a - 1 + zo
                        if 0 <= zi < 2:
                            to[pl.ds(((b * 3 + e) * 2 + zo) * 16, 16), pl.ds(zi * 128, 128)] = tile


def half_of():
    return lax.rem(lax.axis_index("ch") // 2, 2)


def aligned(total, lane):
    before = jnp.where(lane == 0, 0.0, pltpu.roll(total[0:32], 1, 1))
    after = jnp.where(lane == 127, 0.0, pltpu.roll(total[64:96], 127, 1))
    return total[32:64] + (before + after)


def inner_kernel(mine, theirs, taps, taps2, pre, pre2, sums):
    half = half_of()
    lane = lanes_of((32, 128))

    def row_of(row):
        return jnp.concatenate(
            [held[chip, z * 17 + row + half] for z in range(2) for chip in range(4) for held in (mine, theirs)],
            axis=0,
        )

    near = jnp.concatenate(
        [held[chip, z * 17 + 16 * (1 - half)] for z in range(2) for chip in range(4) for held in (mine, theirs)],
        axis=0,
    )
    ends = [
        [aligned(jnp.dot(w[pl.ds(b * 96, 96)], near, preferred_element_type=F32), lane) for b in (0, 2)]
        for w in (taps, taps2)
    ]
    for p in range(8):
        pair = jnp.concatenate([row_of(2 * p), row_of(2 * p + 1)], axis=1)
        for t, (weights, to) in enumerate(((taps, pre), (taps2, pre2))):
            got = jnp.dot(weights[...], pair, preferred_element_type=F32)
            for h in range(2):
                for b in range(3):
                    row = 2 * p + h + 1 - b
                    if not 0 <= row < 16:
                        continue
                    part = got[b * 96 : (b + 1) * 96, h * 128 : (h + 1) * 128]
                    if not (b == 0 or (b == 1 and row == 0)):
                        part = part + sums[t, row]
                    if b == 2 or (b == 1 and row == 15):
                        total = aligned(part, lane)
                        if row == 0:
                            total = total + jnp.where(half == 1, ends[t][0], 0.0)
                        if row == 15:
                            total = total + jnp.where(half == 0, ends[t][1], 0.0)
                        to[row] = total
                    else:
                        sums[t, row] = part


def outer_kernel(pre, taps, halo, filters, out, flat):
    me = lax.axis_index("ch")
    half, core = half_of(), lax.rem(me, 2)
    parts = filters[pl.ds(432, 16)].astype(F32)
    offset = (parts[:, 0:1] + parts[:, 1:2]) + parts[:, 2:3]
    offset = jnp.concatenate([offset, offset], axis=0)
    sources = [2 * chip + (core ^ t) for chip in range(4) for t in range(2)]
    lane24 = lanes_of((24, 128))
    total = [[jnp.zeros((24, 128), F32) for _ in range(2)] for _ in range(2)]
    for j, source in enumerate(sources):
        both = halo[source, pl.ds(32, 16)].astype(F32)
        both = jnp.concatenate([both, pltpu.roll(both[8:16], 64, 1)], axis=0)
        for side in range(2):
            for z in range(2):
                shift = (j * 16 - side * 32 - z * 16) % 128
                piece = pltpu.roll(both, shift, 1) if shift else both
                total[side][z] = jnp.where(lane24 // 16 == j, piece, total[side][z])
    beside = jnp.concatenate(
        [jnp.concatenate(total[0], axis=1), jnp.concatenate(total[1], axis=1), jnp.zeros((80, 256), F32)], axis=0
    ).astype(BF)
    edge = lax.dot_general(taps[...], beside, (((1,), (1,)), ((), ())), preferred_element_type=F32)
    before, after = (
        edge[e * 32 : e * 32 + 32]
        + pltpu.roll(edge[96 + e * 32 : 128 + e * 32], 127, 1)
        + pltpu.roll(edge[192 + e * 32 : 224 + e * 32], 126, 1)
        for e in (0, 2)
    )
    lane = lanes_of((32, 128))
    far = jnp.concatenate(
        [halo[source, pl.ds(z * 16, 16)] for z in range(2) for source in sources], axis=0
    ).astype(F32)
    far = far.astype(BF)
    ends = [
        aligned(jnp.dot(taps[pl.ds(b * 96, 96)], far, preferred_element_type=F32), lane) for b in (0, 2)
    ]
    above = jnp.where(half == 0, ends[0], 0.0)
    below = jnp.where(half == 1, ends[1], 0.0)
    for row in range(16):
        total = pre[row] + offset
        if row == 0:
            total = total + above
        if row == 15:
            total = total + below
        total = total + jnp.where(lane == 0, before[:, row : row + 1], 0.0)
        total = total + jnp.where(lane == 127, after[:, 24 + row : 25 + row], 0.0)
        total = jnp.where(total >= 0, total, 0.3 * total)
        for z in range(2):
            flat[pl.ds(z * 16 + row, 16, stride=32), :] = total[z * 16 : z * 16 + 16]
    out[...] = flat[...].reshape(16, 2, 16, 128).astype(BF)


def place(ready, out, start, sem):
    copy = pltpu.make_async_copy(ready, out.at[:, :, pl.ds(pl.multiple_of(start, 16), 16)], sem)
    copy.start()
    copy.wait()


def kept_kernel(pre, taps, halo, filters, out, flat, ready, sem):
    outer_kernel(pre, taps, halo, filters, ready, flat)
    place(ready, out, 16 * half_of(), sem)


def unpack_kernel(got, held, out, sem):
    place(got, out, 16 * (1 - half_of()), sem)


def shifts(array, axis, up=True):
    size = lax.axis_size(axis)
    pairs = [(i, i + 1) for i in range(size - 1)]
    return lax.ppermute(array, axis, pairs if up else [(j, i) for i, j in pairs])


def swapped(array, t):
    return lax.ppermute(array, "ch", [(d, d ^ t) for d in range(8)])


def thirds(bias):
    high = bias.astype(BF)
    rest = bias - high.astype(F32)
    middle = rest.astype(BF)
    low = (rest - middle.astype(F32)).astype(BF)
    return jnp.pad(jnp.stack([high, middle, low], axis=1), ((0, 0), (0, 125)))


def stages(volume, weights, bias):
    cols = call(columns_kernel, shaped(32, 128), [], volume, moved=1 << 19)
    blocks, first, last = call(
        pack_kernel,
        [shaped(4, 34, 16, 128), shaped(32, 128), shaped(32, 128)],
        [pltpu.VMEM((1024, 128), F32)],
        volume,
        moved=1 << 20,
    )
    mine = lax.all_to_all(blocks, "ch", split_axis=0, concat_axis=0, tiled=True, axis_index_groups=CORES)
    left = shifts(cols, "sy", True)
    right = shifts(cols, "sy", False)
    own = jnp.concatenate([weights.transpose(2, 3, 4, 0, 1).reshape(432, 128), thirds(bias)], axis=0)
    other = swapped(own, 2)
    up, down, beside = call(
        beside_kernel,
        [shaped(48, 128), shaped(48, 128), shaped(32, 128, dtype=F32)],
        [],
        first,
        last,
        left,
        right,
        moved=1 << 16,
    )
    above = shifts(up, "sx", True)
    below = shifts(down, "sx", False)
    theirs = swapped(mine, 1)
    taps, taps2 = call(taps_kernel, [shaped(288, 256)] * 2, [], own, other, moved=1 << 19)
    halo = call(halo_kernel, shaped(8, 48, 128), [pltpu.VMEM((40, 128), F32)], above, below, beside, moved=1 << 17)
    halo = lax.all_to_all(halo, "ch", split_axis=0, concat_axis=0, tiled=True)
    pre, pre2 = call(
        inner_kernel,
        [shaped(16, 32, 128, dtype=F32)] * 2,
        [pltpu.VMEM((2, 16, 96, 128), F32)],
        mine,
        theirs,
        taps,
        taps2,
        flops=2 * 576 * 256 * 2048,
        moved=3 << 20,
    )
    cost = dict(flops=2 * 288 * 256 * 256, moved=1 << 20)
    flat = pltpu.VMEM((512, 128), F32)
    ready, sem = pltpu.VMEM((16, 2, 16, 128), BF), pltpu.SemaphoreType.DMA
    space = pl.BlockSpec(memory_space=pl.ANY)
    sent = call(outer_kernel, shaped(16, 2, 16, 128), [flat], pre2, taps2, halo, other, **cost)
    got = swapped(sent, 2)
    result = call(kept_kernel, shaped(16, 2, 32, 128), [flat, ready, sem], pre, taps, halo, own, place=space, **cost)
    return call(unpack_kernel, shaped(16, 2, 32, 128), [sem], got, result, moved=1 << 18, place=space, shared={1: 0})


def solution(mesh):
    in_specs = (P("ch", None, "sx", "sy"), P("ch", None, None, None, None), P("ch"))
    out_specs = P("ch", None, "sx", "sy")
    return jax.shard_map(stages, mesh=mesh, in_specs=in_specs, out_specs=out_specs, check_vma=False)
```
